128 devices in a mesh: tok: 32 (over y, x, core), head: 4 (over z).
Axes of the slice: x: 4, y: 4, z: 4, core: 2. Of those that a mesh axis runs over, the one named last changes fastest.
Arguments:
- layer_input: bfloat16 [16384, 5120], P('tok', 'head'), may hold values from -6 to 6
- rate_weight: bfloat16 [5120, 12], P('head'), may hold values from -0.078125 to 0.078125
- token_queries: bfloat16 [16384, 3072], P('tok', 'head'), may hold values from -80 to 80
- token_keys: bfloat16 [16384, 3072], P('tok', 'head'), may hold values from -5 to 5
- token_values: bfloat16 [16384, 3072], P('tok', 'head'), may hold values from -6 to 6
- first_weight: float32 [12, 256, 512], P('head'), may hold values from -0.375 to 0.375
- third_weight: float32 [12, 256, 512], P('head'), may hold values from -0.375 to 0.375
- second_weight: float32 [12, 512, 256], P('head'), may hold values from -0.25 to 0.25
- update_scale: float32 [12], P('head'), may hold values from 0.5 to 2
- out_gain: float32 [3072], P('head'), may hold values from 0.25 to 1.75
Outputs:
- mixed: bfloat16 [16384, 3072], P('tok', 'head')
The draws below stay inside these ranges and needn't reach their ends.
All inputs are finite; a program needn't handle non-finite values.
Results may differ from the reference program's by a relative error of at most 0.033.
Values may be sent and summed in bfloat16 or wider, within the bound.
A program may use at most 128 MiB of HBM per device.

```python
import math
import jax
import jax.numpy as jnp
from jax import lax

D = 5120
HEADS = 12
HDIM = 256
FFN = 512
WINDOW = 256
STEPS = 5
TOKENS = 16384


def query_key_pair(key):
    base = jax.random.fold_in(key, 7311)
    first, second = jax.random.split(base, 2)
    shape = (TOKENS, HEADS * HDIM)
    drawn_keys = jnp.clip(jax.random.normal(first, shape, jnp.float32), -4.5, 4.5)
    drawn_queries = jnp.clip(jax.random.normal(second, shape, jnp.float32), -4.5, 4.5)
    return (drawn_queries, drawn_keys)


def draw_token_queries(key, part):
    return query_key_pair(key)[0].astype(jnp.bfloat16)


def draw_token_keys(key, part):
    return query_key_pair(key)[1].astype(jnp.bfloat16)


def block_scale(stream_key, dims, cuts, smallest, largest):
    factor_of = 1.0
    for axis_at, shards_of in cuts:
        draws = jax.random.uniform(jax.random.fold_in(jax.random.fold_in(stream_key, 6), axis_at), (shards_of,), jnp.float32, smallest / len(cuts), largest / len(cuts))
        factor_of = factor_of * jnp.repeat(jnp.exp(draws), dims[axis_at] // shards_of).reshape((-1,) + (1,) * (len(dims) - 1 - axis_at))
    return factor_of


def normal_values(stream_key, dims, width, most, pieces=(), held_as=jnp.bfloat16):
    values = width * jax.random.normal(stream_key, dims, jnp.float32)
    if pieces:
        values = values * block_scale(stream_key, dims, pieces, -0.22, 0.18)
    return jnp.clip(values, -most, most).astype(held_as)


def setup_inputs(seed: int = 0) -> dict:
    streams_of = jax.random.split(jax.random.key(seed), 11)
    layer_input = normal_values(streams_of[0], (TOKENS, D), 1.0, 6.0, ((0, 32), (1, 4)))
    rate_weight = normal_values(streams_of[1], (D, HEADS), D ** -0.5, 0.078125, ((0, 4),))
    token_queries = draw_token_queries(jax.random.fold_in(streams_of[10], 71), 0)
    token_keys = draw_token_keys(jax.random.fold_in(streams_of[10], 71), 0)
    token_values = normal_values(streams_of[4], (TOKENS, HEADS * HDIM), 1.0, 6.0, ((0, 32), (1, 4)))
    first_weight = normal_values(streams_of[5], (HEADS, HDIM, FFN), HDIM ** -0.5, 0.375, ((0, 4),), jnp.float32)
    third_weight = normal_values(streams_of[6], (HEADS, HDIM, FFN), HDIM ** -0.5, 0.375, ((0, 4),), jnp.float32)
    second_weight = normal_values(streams_of[7], (HEADS, FFN, HDIM), FFN ** -0.5, 0.25, ((0, 4),), jnp.float32)
    update_scale = jnp.clip(jnp.exp(math.log(2.0) - 1.3862944 * jax.random.uniform(streams_of[8], (HEADS,), jnp.float32) ** block_scale(streams_of[8], (HEADS,), ((0, 4),), -0.2, 0.2)), 0.5, 2.0)
    out_gain = jnp.clip(1.0 + 0.15 * jax.random.normal(streams_of[9], (HEADS * HDIM,), jnp.float32), 0.25, 1.75)
    return {"layer_input": layer_input, "rate_weight": rate_weight, "token_queries": token_queries, "token_keys": token_keys, "token_values": token_values, "first_weight": first_weight, "third_weight": third_weight, "second_weight": second_weight, "update_scale": update_scale, "out_gain": out_gain}


COEF_A = 3.4445
COEF_B = -4.775
COEF_C = 2.0315
EPS_SCALE = 1e-07
EPS_RMS = 1e-06

def fast_gradient(inputs):
    key_head, value_head, rate_head, first_head, third_head, second_head = inputs
    first_half = first_head.astype(jnp.bfloat16)
    third_half = third_head.astype(jnp.bfloat16)
    second_half = second_head.astype(jnp.bfloat16)
    gate_pre = jnp.dot(key_head, first_half, preferred_element_type=jnp.float32)
    up_pre = jnp.dot(key_head, third_half, preferred_element_type=jnp.float32)
    sigmoid_gate = jax.nn.sigmoid(gate_pre)
    activated = gate_pre * sigmoid_gate
    hidden = (activated * up_pre).astype(jnp.bfloat16)
    weighted = (value_head.astype(jnp.float32) * rate_head[:, None]).astype(jnp.bfloat16)
    hidden_grad = -jnp.dot(weighted, second_half.T, preferred_element_type=jnp.float32)
    gate_grad = (hidden_grad * up_pre * sigmoid_gate * (1.0 + gate_pre * (1.0 - sigmoid_gate))).astype(jnp.bfloat16)
    up_grad = (hidden_grad * activated).astype(jnp.bfloat16)
    first_grad = jnp.dot(key_head.T, gate_grad, preferred_element_type=jnp.float32)
    third_grad = jnp.dot(key_head.T, up_grad, preferred_element_type=jnp.float32)
    second_grad = -jnp.dot(weighted.T, hidden, preferred_element_type=jnp.float32)
    return (first_grad, third_grad, second_grad)

def orthogonalize(stacked):
    scale = jnp.sqrt(lax.optimization_barrier(jnp.sum(stacked * stacked, axis=(1, 2))))
    iterate = (stacked / (scale[:, None, None] + EPS_SCALE)).astype(jnp.bfloat16)
    for repeat in range(STEPS):
        wide = iterate.astype(jnp.float32)
        gram_half = jnp.einsum('mik,mjk->mij', wide, wide, precision=lax.Precision.HIGHEST).astype(jnp.bfloat16)
        gram_wide = gram_half.astype(jnp.float32)
        squared = jnp.einsum('mij,mjk->mik', gram_wide, gram_wide, precision=lax.Precision.HIGHEST)
        mixing = (COEF_B * gram_wide + COEF_C * squared).astype(jnp.bfloat16)
        moved = jnp.einsum('mij,mjk->mik', mixing.astype(jnp.float32), wide, precision=lax.Precision.HIGHEST)
        iterate = (COEF_A * wide + moved).astype(jnp.bfloat16)
    return iterate

def fast_apply(query_head, first_head, third_head, second_head, gain_head):
    gate_pre = jnp.dot(query_head, first_head.astype(jnp.bfloat16), preferred_element_type=jnp.float32)
    up_pre = jnp.dot(query_head, third_head.astype(jnp.bfloat16), preferred_element_type=jnp.float32)
    hidden = (gate_pre * jax.nn.sigmoid(gate_pre) * up_pre).astype(jnp.bfloat16)
    output = jnp.dot(hidden, second_head.astype(jnp.bfloat16), preferred_element_type=jnp.float32)
    return output * lax.rsqrt(lax.optimization_barrier(jnp.mean(output * output, axis=-1, keepdims=True)) + EPS_RMS) * gain_head

def window_attention(query_head, key_head, value_head):
    block_rows = min(512, TOKENS)
    padded_keys = jnp.concatenate([jnp.zeros((WINDOW, HDIM), key_head.dtype), key_head])
    padded_values = jnp.concatenate([jnp.zeros((WINDOW, HDIM), value_head.dtype), value_head])
    starts = jnp.arange(TOKENS // block_rows, dtype=jnp.int32) * block_rows

    def one_block(start):
        query_block = lax.dynamic_slice_in_dim(query_head, start, block_rows, 0)
        key_block = lax.dynamic_slice_in_dim(padded_keys, start, block_rows + WINDOW, 0)
        value_block = lax.dynamic_slice_in_dim(padded_values, start, block_rows + WINDOW, 0)
        query_place = start + jnp.arange(block_rows, dtype=jnp.int32)
        key_place = start - WINDOW + jnp.arange(block_rows + WINDOW, dtype=jnp.int32)
        scores = jnp.dot(query_block, key_block.T, preferred_element_type=jnp.float32) * HDIM ** (-0.5)
        allowed = (key_place[None, :] <= query_place[:, None]) & (key_place[None, :] > query_place[:, None] - WINDOW) & (key_place[None, :] >= 0)
        scores = jnp.where(allowed, scores, -1e+30)
        highest = lax.optimization_barrier(jnp.max(scores, axis=-1, keepdims=True))
        weights = jnp.exp(scores - highest)
        shares = (weights / lax.optimization_barrier(jnp.sum(weights, axis=-1, keepdims=True))).astype(jnp.bfloat16)
        return jnp.dot(shares, value_block, preferred_element_type=jnp.float32)
    return lax.map(one_block, starts).reshape(TOKENS, HDIM)

def reference(layer_input, rate_weight, token_queries, token_keys, token_values, first_weight, third_weight, second_weight, update_scale, out_gain):
    token_rates = jax.nn.softplus(jnp.dot(layer_input, rate_weight, preferred_element_type=jnp.float32))

    def by_head(array):
        return array.reshape(TOKENS, HEADS, HDIM).transpose(1, 0, 2)
    query_heads = by_head(token_queries)
    key_heads = by_head(token_keys)
    value_heads = by_head(token_values)
    first_grad, third_grad, second_grad = lax.map(fast_gradient, (key_heads, value_heads, token_rates.T, first_weight, third_weight, second_weight))
    stacked = jnp.concatenate([first_grad, third_grad, second_grad], axis=0)
    ortho = orthogonalize(stacked).astype(jnp.float32)
    step_size = update_scale[:, None, None]
    new_first = first_weight - step_size * ortho[:HEADS]
    new_third = third_weight - step_size * ortho[HEADS:2 * HEADS]
    new_second = second_weight - step_size * jnp.swapaxes(ortho[2 * HEADS:], 1, 2)
    gains = out_gain.reshape(HEADS, HDIM)

    def head_output(inputs):
        query_head, key_head, value_head, first_head, third_head, second_head, gain_head = inputs
        normed = fast_apply(query_head, first_head, third_head, second_head, gain_head)
        return normed + window_attention(query_head, key_head, value_head)
    outputs = lax.map(head_output, (query_heads, key_heads, value_heads, new_first, new_third, new_second, gains))
    return outputs.transpose(1, 0, 2).reshape(TOKENS, HEADS * HDIM).astype(jnp.bfloat16)
```

```python
import functools

import jax
import jax.numpy as jnp
from jax import lax
from jax.experimental import pallas as pl
from jax.experimental.pallas import tpu as pltpu
from jax.sharding import PartitionSpec as P

MESH = pl.DeviceIdType.MESH
HDIM = 256
FFN = 512
HALF = 128
ROWS = 512
HEADS = 3
MATS = 9
STEPS = 5
COEF_A = 3.4445
COEF_B = -4.775
COEF_C = 2.0315
EPS_SCALE = 1e-07
EPS_RMS = 1e-06
F32 = jnp.float32
BF16 = jnp.bfloat16

PLACE = [(m % 2, m // 2, m % 2) for m in range(8)] + [(0, 0, 2)]


def dot(a, b):
    return jnp.dot(a, b, preferred_element_type=F32)


def dot_nt(a, b):
    return lax.dot_general(a, b, (((1,), (1,)), ((), ())), preferred_element_type=F32)


def kernel(
    x_hbm, rw_hbm, q_hbm, k_hbm, v_hbm, w1_hbm, w3_hbm, w2_hbm, scale_ref, gain_ref, out_ref,
    xin, rw, q, k, v, w1, w3, w2, load_sem,
    lpad, lg, lrx, lss, lrs,
    hk, hv, hss, hrs,
    pg, pu, hd, kt, vt, att,
    gown, gs0, rx0, gs1, rx1, gs2, rx2, gfull, oall,
    ss0, rs0, ss1, rs1, ss2, rs2, ssx, rsx, ss3, rs3, ss4, rs4,
):
    tok = lax.axis_index("tok")
    z = lax.axis_index("head")
    c = lax.rem(tok, 2)
    x = lax.rem(lax.div(tok, 2), 4)
    y = lax.div(tok, 8)
    where = (x, y)

    def on_axis(axis, place):
        if axis == 0:
            return ((y * 4 + place) * 2 + c, z)
        return ((place * 4 + x) * 2 + c, z)

    sibling = (tok + 1 - 2 * c, z)

    def remote(src, dst, send, recv, device):
        return pltpu.make_async_remote_copy(
            src_ref=src, dst_ref=dst, send_sem=send, recv_sem=recv, device_id=device, device_id_type=MESH
        )

    loads = [
        pltpu.make_async_copy(a, b, load_sem.at[i])
        for i, (a, b) in enumerate(
            [(x_hbm, xin), (rw_hbm, rw), (k_hbm, k), (v_hbm, v), (w1_hbm, w1), (w3_hbm, w3), (w2_hbm, w2), (q_hbm, q)]
        )
    ]
    for load in loads:
        load.start()

    barrier = pltpu.get_barrier_semaphore()

    def greet(device):
        pl.semaphore_signal(barrier, inc=1, device_id=device, device_id_type=MESH)

    greet(sibling)
    for d in range(1, 4):
        greet(on_axis(0, lax.rem(x + d, 4)))
        greet(on_axis(1, lax.rem(y + d, 4)))
        greet((tok, lax.rem(z + d, 4)))

    greet((lax.rem(tok + 31, 32), z))
    greet((lax.rem(tok + 1, 32), z))

    lpad[...] = jnp.zeros_like(lpad)
    lg[...] = jnp.zeros_like(lg)
    gfull[2] = jnp.zeros((HDIM, FFN), BF16)
    loads[0].wait()
    loads[1].wait()
    lpad[:, 0:12] = dot(xin[...], rw[...])
    turned = lpad[...].T
    for head in range(4):
        lg[head, 0:HEADS, :] = turned[HEADS * head : HEADS * (head + 1)]
    loads[2].wait()
    loads[3].wait()

    pl.semaphore_wait(barrier, 12)

    logit_copies = []
    for d in range(1, 4):
        there = lax.rem(z + d, 4)
        copy = remote(lg.at[there], lrx.at[d - 1], lss.at[d - 1], lrs.at[d - 1], (tok, there))
        copy.start()
        logit_copies.append(copy)

    halo = [
        remote(k.at[pl.ds(ROWS - HDIM, HDIM)], hk, hss.at[0], hrs.at[0], (tok + 1, z)),
        remote(v.at[pl.ds(ROWS - HDIM, HDIM)], hv, hss.at[1], hrs.at[1], (tok + 1, z)),
    ]

    @pl.when(tok < 31)
    def _():
        for copy in halo:
            copy.start()

    @pl.when(tok == 0)
    def _():
        hk[...] = jnp.zeros_like(hk)
        hv[...] = jnp.zeros_like(hv)

    for load in loads[4:7]:
        load.wait()

    def before_rates(h, carry):
        columns = pl.ds(pl.multiple_of(h * HDIM, HDIM), HDIM)
        first = w1[h].astype(BF16)
        third = w3[h].astype(BF16)
        second = w2[h].astype(BF16)
        for part in range(2):
            rows = pl.ds(part * HDIM, HDIM)
            keys = k[rows, columns]
            values = v[rows, columns]
            kt[h, :, rows] = keys.T
            vt[h, :, rows] = values.T
            gate = dot(keys, first)
            up = dot(keys, third)
            back = -dot_nt(values, second)
            sig = jax.nn.sigmoid(gate)
            activ = gate * sig
            pg[h, rows, :] = back * up * sig * (1.0 + gate * (1.0 - sig))
            pu[h, rows, :] = back * activ
            hd[h, rows, :] = -(activ * up)
        return carry

    lax.fori_loop(0, HEADS, before_rates, 0)

    for copy in logit_copies:
        copy.wait_recv()
    logits = lg[z] + lrx[0] + lrx[1] + lrx[2]
    rates = jnp.maximum(logits, 0.0) + jnp.log1p(jnp.exp(-jnp.abs(logits)))
    rates_down = rates.T

    mine = pl.ds(pl.multiple_of(c * HALF, HALF), HALF)
    other = pl.ds(pl.multiple_of(HALF - c * HALF, HALF), HALF)

    s0 = [
        remote(gs0.at[m], rx0.at[m], ss0.at[m], rs0.at[m], sibling) for m in range(MATS)
    ]
    s1 = []
    for m in range(MATS):
        axis, place, slot = PLACE[m]
        step = lax.rem(place - where[axis] + 4, 4)
        index = jnp.maximum(step - 1, 0)
        s1.append(
            remote(gs1.at[m], rx1.at[slot, index], ss1.at[m], rs1.at[slot, index], on_axis(axis, place))
        )

    def send_chip_sum(m):
        axis, place, slot = PLACE[m]
        s0[m].wait_recv()
        both = gown[m] + rx0[m].astype(F32)
        gown[m] = both
        gs1[m] = both.astype(BF16)

        @pl.when(where[axis] != place)
        def _():
            s1[m].start()

    for h in range(HEADS):
        rate = rates_down[:, h : h + 1]
        wides = ((kt, pg), (kt, pu), (vt, hd))
        for j, (left, right) in enumerate(wides):
            m = 3 * h + j
            scaled = (rate * right[h]).astype(BF16)
            gs0[m] = dot(left[h, other, :], scaled).astype(BF16)
            s0[m].start()
            gown[m] = dot(left[h, mine, :], scaled)
            if m > 1:
                send_chip_sum(m - 2)
    send_chip_sum(MATS - 2)
    send_chip_sum(MATS - 1)

    loads[7].wait()

    @pl.when(tok > 0)
    def _():
        for copy in halo:
            copy.wait_recv()

    row = lax.broadcasted_iota(jnp.int32, (HDIM, HDIM), 0)
    column = lax.broadcasted_iota(jnp.int32, (HDIM, HDIM), 1)
    has_past = tok > 0

    def attend(h, carry):
        columns = pl.ds(pl.multiple_of(h * HDIM, HDIM), HDIM)
        low, high = pl.ds(0, HDIM), pl.ds(HDIM, HDIM)
        blocks = (
            (low, hk[:, columns], hv[:, columns], k[low, columns], v[low, columns], True),
            (high, k[low, columns], v[low, columns], k[high, columns], v[high, columns], False),
        )
        for rows, old_k, old_v, new_k, new_v, edge in blocks:
            queries = q[rows, columns]
            seen = column > row
            if edge:
                seen = jnp.logical_and(seen, has_past)
            old = jnp.where(seen, dot_nt(queries, old_k) * HDIM ** (-0.5), -1e30)
            new = jnp.where(column <= row, dot_nt(queries, new_k) * HDIM ** (-0.5), -1e30)
            top = jnp.maximum(jnp.max(old, axis=1, keepdims=True), jnp.max(new, axis=1, keepdims=True))
            old = jnp.exp(old - top)
            new = jnp.exp(new - top)
            total = jnp.sum(old, axis=1, keepdims=True) + jnp.sum(new, axis=1, keepdims=True)
            mixed = dot(old.astype(BF16), old_v) + dot(new.astype(BF16), new_v)
            att[rows, columns] = mixed / total
        return carry

    lax.fori_loop(0, HEADS, attend, 0)

    owned = (2 * x, 2 * y + 1, 8)
    second_copies = []
    for slot in range(3):
        axis = (0, 1, 0)[slot]
        second_copies.append(
            [
                remote(
                    gs2.at[slot], rx2.at[slot, d - 1], ss2.at[slot, d - 1], rs2.at[slot, d - 1],
                    on_axis(1 - axis, lax.rem(where[1 - axis] + d, 4)),
                )
                for d in range(1, 4)
            ]
        )
    third_copies = [
        [
            remote(
                oall.at[owned[slot], mine], oall.at[owned[slot], mine], ss3.at[slot, d - 1], rs3.at[owned[slot]],
                on_axis((0, 1, 0)[slot], lax.rem(where[(0, 1, 0)[slot]] + d, 4)),
            )
            for d in range(1, 4)
        ]
        for slot in range(3)
    ]
    half_copies = [
        remote(gfull.at[slot, mine], gfull.at[slot, mine], ssx.at[slot], rsx.at[slot], sibling) for slot in range(3)
    ]

    def if_there(slot, action):
        if slot < 2:
            action()
        else:
            pl.when(x == 0)(action)

    def arrived_first(slot):
        m = owned[slot]
        total = gown[m]
        for d in range(3):
            remote(gs1.at[m], rx1.at[slot, d], ss1.at[m], rs1.at[slot, d], sibling).wait_recv()
            total = total + rx1[slot, d].astype(F32)
        gown[m] = total
        gs2[slot] = total.astype(BF16)
        for copy in second_copies[slot]:
            copy.start()

    def arrived_second(slot):
        total = gown[owned[slot]]
        for d, copy in enumerate(second_copies[slot]):
            copy.wait_recv()
            total = total + rx2[slot, d].astype(F32)
        gfull[slot, mine, :] = total.astype(BF16)
        half_copies[slot].start()

    for slot in range(3):
        if_there(slot, functools.partial(arrived_first, slot))
    for slot in range(3):
        if_there(slot, functools.partial(arrived_second, slot))
    for slot in range(3):
        if_there(slot, half_copies[slot].wait_recv)

    iterates = []
    for slot in range(3):
        full = gfull[slot].astype(F32)
        norm = jnp.sqrt(jnp.sum(full * full, keepdims=True)) + EPS_SCALE
        iterates.append((full / norm).astype(BF16))
    for repeat in range(STEPS):
        grams = [dot_nt(it, it).astype(BF16) for it in iterates]
        mixing = [
            (COEF_B * gram.astype(F32) + COEF_C * dot(gram, gram)).astype(BF16) for gram in grams
        ]
        iterates = [
            (COEF_A * it.astype(F32) + dot(mix, it)).astype(BF16) for mix, it in zip(mixing, iterates)
        ]

    def publish(slot):
        oall[owned[slot]] = iterates[slot]
        for copy in third_copies[slot]:
            copy.start()

    for slot in range(3):
        if_there(slot, functools.partial(publish, slot))

    fourth_copies = [
        remote(oall.at[m, mine], oall.at[m, mine], ss4.at[m], rs4.at[m], sibling) for m in range(MATS)
    ]

    def foreign(m, action):
        axis, place, slot = PLACE[m]
        pl.when(where[axis] != place)(action)

    def forward(m):
        def action():
            remote(oall.at[m, mine], oall.at[m, mine], ss4.at[m], rs3.at[m], sibling).wait_recv()
            fourth_copies[m].start()

        foreign(m, action)

    def apply(h):
        for j in range(3):
            foreign(3 * h + j, fourth_copies[3 * h + j].wait_recv)
        columns = pl.ds(h * HDIM, HDIM)
        size = scale_ref[h]
        first = (w1[h] - size * oall[3 * h].astype(F32)).astype(BF16)
        third = (w3[h] - size * oall[3 * h + 1].astype(F32)).astype(BF16)
        second = (w2[h] - size * oall[3 * h + 2].astype(F32).T).astype(BF16)
        gain = gain_ref[:, h * HDIM : (h + 1) * HDIM]
        for part in range(2):
            rows = pl.ds(part * HDIM, HDIM)
            queries = q[rows, columns]
            gate = dot(queries, first)
            up = dot(queries, third)
            hidden = (gate * jax.nn.sigmoid(gate) * up).astype(BF16)
            fast = dot(hidden, second)
            spread = jnp.mean(fast * fast, axis=1, keepdims=True)
            normed = fast * lax.rsqrt(spread + EPS_RMS) * gain
            out_ref[rows, columns] = (att[rows, columns] + normed).astype(BF16)

    for m in range(MATS):
        forward(m)
    for h in range(HEADS):
        apply(h)

    for copy in logit_copies + s0:
        copy.wait_send()

    @pl.when(tok < 31)
    def _():
        for copy in halo:
            copy.wait_send()

    for m in range(MATS):
        foreign(m, s1[m].wait_send)
        foreign(m, fourth_copies[m].wait_send)
    for slot in range(3):

        def finish(slot=slot):
            for copy in second_copies[slot] + [half_copies[slot]] + third_copies[slot]:
                copy.wait_send()

        if_there(slot, finish)


def on_device(x, rw, q, k, v, w1, w3, w2, scale, gain):
    anywhere = pl.BlockSpec(memory_space=pl.ANY)
    dma = pltpu.SemaphoreType.DMA
    features = x.shape[1]
    wide = HEADS * HDIM
    return pl.pallas_call(
        kernel,
        name="layer",
        out_shape=jax.ShapeDtypeStruct((ROWS, wide), BF16),
        in_specs=[anywhere] * 8
        + [pl.BlockSpec(memory_space=pltpu.SMEM), pl.BlockSpec(memory_space=pltpu.VMEM)],
        out_specs=pl.BlockSpec(memory_space=pltpu.VMEM),
        scratch_shapes=[
            pltpu.VMEM((ROWS, features), BF16),
            pltpu.VMEM(rw.shape, BF16),
            pltpu.VMEM((ROWS, wide), BF16),
            pltpu.VMEM((ROWS, wide), BF16),
            pltpu.VMEM((ROWS, wide), BF16),
            pltpu.VMEM((HEADS, HDIM, FFN), F32),
            pltpu.VMEM((HEADS, HDIM, FFN), F32),
            pltpu.VMEM((HEADS, FFN, HDIM), F32),
            dma((8,)),
            pltpu.VMEM((ROWS, 128), F32),
            pltpu.VMEM((4, 8, ROWS), F32),
            pltpu.VMEM((3, 8, ROWS), F32),
            dma((3,)),
            dma((3,)),
            pltpu.VMEM((HDIM, wide), BF16),
            pltpu.VMEM((HDIM, wide), BF16),
            dma((2,)),
            dma((2,)),
            pltpu.VMEM((HEADS, ROWS, FFN), F32),
            pltpu.VMEM((HEADS, ROWS, FFN), F32),
            pltpu.VMEM((HEADS, ROWS, FFN), F32),
            pltpu.VMEM((HEADS, HDIM, ROWS), BF16),
            pltpu.VMEM((HEADS, HDIM, ROWS), BF16),
            pltpu.VMEM((ROWS, wide), F32),
            pltpu.VMEM((MATS, HALF, FFN), F32),
            pltpu.VMEM((MATS, HALF, FFN), BF16),
            pltpu.VMEM((MATS, HALF, FFN), BF16),
            pltpu.VMEM((MATS, HALF, FFN), BF16),
            pltpu.VMEM((3, 3, HALF, FFN), BF16),
            pltpu.VMEM((3, HALF, FFN), BF16),
            pltpu.VMEM((3, 3, HALF, FFN), BF16),
            pltpu.VMEM((3, HDIM, FFN), BF16),
            pltpu.VMEM((MATS, HDIM, FFN), BF16),
            dma((MATS,)),
            dma((MATS,)),
            dma((MATS,)),
            dma((3, 3)),
            dma((3, 3)),
            dma((3, 3)),
            dma((3,)),
            dma((3,)),
            dma((3, 3)),
            dma((MATS,)),
            dma((MATS,)),
            dma((MATS,)),
        ],
        compiler_params=pltpu.CompilerParams(
            collective_id=0, has_side_effects=True, vmem_limit_bytes=56 << 20
        ),
    )(x, rw, q, k, v, w1, w3, w2, scale, gain.reshape(1, wide))


def solution(mesh):
    placed = (
        P("tok", "head"),
        P("head", None),
        P("tok", "head"),
        P("tok", "head"),
        P("tok", "head"),
        P("head", None, None),
        P("head", None, None),
        P("head", None, None),
        P("head"),
        P("head"),
    )
    return jax.shard_map(
        on_device, mesh=mesh, in_specs=placed, out_specs=P("tok", "head"), check_vma=False
    )
```

```python
import jax
import jax.numpy as jnp
from jax import lax
from jax.experimental import pallas as pl
from jax.experimental.pallas import tpu as pltpu
from jax.sharding import PartitionSpec as P

MESH = pl.DeviceIdType.MESH
HDIM = 256
FFN = 512
HALF = 128
ROWS = 512
HEADS = 3
MATS = 9
STEPS = 5
COEF_A = 3.4445
COEF_B = -4.775
COEF_C = 2.0315
EPS_SCALE = 1e-07
EPS_RMS = 1e-06
F32 = jnp.float32
BF16 = jnp.bfloat16

PLACE = [None] + [((m - 1) % 2, (m - 1) // 2) for m in range(1, MATS)]
QUARTER = HALF // 4


def dot(a, b):
    return jnp.dot(a, b, preferred_element_type=F32)


def dot_nt(a, b):
    return lax.dot_general(a, b, (((1,), (1,)), ((), ())), preferred_element_type=F32)


def kernel(
    x_hbm, rw_hbm, q_hbm, k_hbm, v_hbm, w1_hbm, w3_hbm, w2_hbm, scale_ref, gain_ref, out_ref,
    xin, rw, q, k, v, w1, w3, w2, load_sem,
    lpad, lg, lrx, lss, lrs,
    hk, hv, hss, hrs,
    pg, pu, hd, kt, vt, att,
    eq, es, erx, ess, ers,
    gown, gs0, rx0, gs1, rx1, gs2, rx2, gfull, oall,
    ss0, rs0, ss1, rs1, ss2, rs2, ssx, rsx, ss3, rs3, ss4, rs4,
):
    tok = lax.axis_index("tok")
    z = lax.axis_index("head")
    c = lax.rem(tok, 2)
    x = lax.rem(lax.div(tok, 2), 4)
    y = lax.div(tok, 8)
    where = (x, y)

    def on_axis(axis, place):
        if axis == 0:
            return ((y * 4 + place) * 2 + c, z)
        return ((place * 4 + x) * 2 + c, z)

    sibling = (tok + 1 - 2 * c, z)

    def remote(src, dst, send, recv, device):
        return pltpu.make_async_remote_copy(
            src_ref=src, dst_ref=dst, send_sem=send, recv_sem=recv, device_id=device, device_id_type=MESH
        )

    loads = [
        pltpu.make_async_copy(a, b, load_sem.at[i])
        for i, (a, b) in enumerate(
            [(x_hbm, xin), (rw_hbm, rw), (k_hbm, k), (v_hbm, v), (w1_hbm, w1), (w3_hbm, w3), (w2_hbm, w2), (q_hbm, q)]
        )
    ]
    for load in loads:
        load.start()

    barrier = pltpu.get_barrier_semaphore()

    def greet(device):
        pl.semaphore_signal(barrier, inc=1, device_id=device, device_id_type=MESH)

    greet(sibling)
    for d in range(1, 4):
        greet(on_axis(0, lax.rem(x + d, 4)))
        greet(on_axis(1, lax.rem(y + d, 4)))
        greet((tok, lax.rem(z + d, 4)))

    greet((lax.rem(tok + 31, 32), z))
    greet((lax.rem(tok + 1, 32), z))

    lpad[...] = jnp.zeros_like(lpad)
    lg[...] = jnp.zeros_like(lg)
    loads[0].wait()
    loads[1].wait()
    lpad[:, 0:12] = dot_nt(xin[...], rw[...])
    turned = lpad[...].T
    for head in range(4):
        lg[head, 0:HEADS, :] = turned[HEADS * head : HEADS * (head + 1)]
    loads[2].wait()
    loads[3].wait()

    pl.semaphore_wait(barrier, 12)

    logit_copies = []
    for d in range(1, 4):
        there = lax.rem(z + d, 4)
        copy = remote(lg.at[there], lrx.at[d - 1], lss.at[d - 1], lrs.at[d - 1], (tok, there))
        copy.start()
        logit_copies.append(copy)

    halo = [
        remote(k.at[pl.ds(ROWS - HDIM, HDIM)], hk, hss.at[0], hrs.at[0], (tok + 1, z)),
        remote(v.at[pl.ds(ROWS - HDIM, HDIM)], hv, hss.at[1], hrs.at[1], (tok + 1, z)),
    ]

    @pl.when(tok < 31)
    def _():
        for copy in halo:
            copy.start()

    @pl.when(tok == 0)
    def _():
        hk[...] = jnp.zeros_like(hk)
        hv[...] = jnp.zeros_like(hv)

    for load in loads[4:7]:
        load.wait()

    def before_rates(h, carry):
        columns = pl.ds(pl.multiple_of(h * HDIM, HDIM), HDIM)
        first = w1[h].astype(BF16)
        third = w3[h].astype(BF16)
        second = w2[h].astype(BF16)
        for part in range(2):
            rows = pl.ds(part * HDIM, HDIM)
            keys = k[rows, columns]
            values = v[rows, columns]
            kt[h, :, rows] = keys.T
            vt[h, :, rows] = values.T
            gate = dot(keys, first)
            up = dot(keys, third)
            back = -dot_nt(values, second)
            sig = jax.nn.sigmoid(gate)
            activ = gate * sig
            pg[h, rows, :] = back * up * sig * (1.0 + gate * (1.0 - sig))
            pu[h, rows, :] = back * activ
            hd[h, rows, :] = -(activ * up)
        return carry

    lax.fori_loop(0, HEADS, before_rates, 0)

    for copy in logit_copies:
        copy.wait_recv()
    logits = lg[z] + lrx[0] + lrx[1] + lrx[2]
    rates = jnp.maximum(logits, 0.0) + jnp.log1p(jnp.exp(-jnp.abs(logits)))
    rates_down = rates.T

    mine = pl.ds(pl.multiple_of(c * HALF, HALF), HALF)
    other = pl.ds(pl.multiple_of(HALF - c * HALF, HALF), HALF)

    s0 = [
        remote(gs0.at[m], rx0.at[m], ss0.at[m], rs0.at[m], sibling) for m in range(MATS)
    ]
    s1 = [None]
    for m in range(1, MATS):
        axis, place = PLACE[m]
        step = lax.rem(place - where[axis] + 4, 4)
        index = jnp.maximum(step - 1, 0)
        s1.append(
            remote(gs1.at[m], rx1.at[axis, index], ss1.at[m], rs1.at[axis, index], on_axis(axis, place))
        )

    def quarter(place):
        return pl.ds(pl.multiple_of(place * QUARTER, QUARTER), QUARTER)

    my_quarter = quarter(c * 4 + x)
    every = [[], [], []]
    for d in (2, 1, 3):
        x_there, y_there = lax.rem(x + d, 4), lax.rem(y + d, 4)
        every[0].append(
            remote(gs1.at[0, quarter(x_there)], erx.at[0, d - 1], ess.at[0, d - 1], ers.at[0, d - 1], on_axis(0, x_there))
        )
        every[1].append(remote(es, erx.at[1, d - 1], ess.at[1, d - 1], ers.at[1, d - 1], on_axis(1, y_there)))
        every[2].append(
            remote(
                gfull.at[2, my_quarter], gfull.at[2, my_quarter], ess.at[2, d - 1], ers.at[2, d - 1], on_axis(0, x_there)
            )
        )

    def send_chip_sum(m):
        s0[m].wait_recv()
        both = gown[m] + rx0[m].astype(F32)
        gown[m] = both
        gs1[m] = both.astype(BF16)
        if m == 0:
            for copy in every[0]:
                copy.start()
            return
        axis, place = PLACE[m]

        @pl.when(where[axis] != place)
        def _():
            s1[m].start()

    for h in range(HEADS):
        rate = rates_down[:, h : h + 1]
        wides = ((kt, pg), (kt, pu), (vt, hd))
        for j, (left, right) in enumerate(wides):
            m = 3 * h + j
            scaled = (rate * right[h]).astype(BF16)
            gs0[m] = dot(left[h, other, :], scaled).astype(BF16)
            s0[m].start()
            gown[m] = dot(left[h, mine, :], scaled)
            if m > 1:
                send_chip_sum(m - 2)
    send_chip_sum(MATS - 2)
    send_chip_sum(MATS - 1)

    for copy in every[0]:
        copy.wait_recv()
    total = gown[0, quarter(x), :] + erx[0, 0].astype(F32) + erx[0, 1].astype(F32) + erx[0, 2].astype(F32)
    eq[...] = total
    es[...] = total.astype(BF16)
    for copy in every[1]:
        copy.start()

    loads[7].wait()

    @pl.when(tok > 0)
    def _():
        for copy in halo:
            copy.wait_recv()

    row = lax.broadcasted_iota(jnp.int32, (HDIM, HDIM), 0)
    column = lax.broadcasted_iota(jnp.int32, (HDIM, HDIM), 1)
    has_past = tok > 0

    def attend(h, carry):
        columns = pl.ds(pl.multiple_of(h * HDIM, HDIM), HDIM)
        low, high = pl.ds(0, HDIM), pl.ds(HDIM, HDIM)
        blocks = (
            (low, hk[:, columns], hv[:, columns], k[low, columns], v[low, columns], True),
            (high, k[low, columns], v[low, columns], k[high, columns], v[high, columns], False),
        )
        for rows, old_k, old_v, new_k, new_v, edge in blocks:
            queries = q[rows, columns]
            seen = column > row
            if edge:
                seen = jnp.logical_and(seen, has_past)
            old = jnp.where(seen, dot_nt(queries, old_k) * HDIM ** (-0.5), -1e30)
            new = jnp.where(column <= row, dot_nt(queries, new_k) * HDIM ** (-0.5), -1e30)
            top = jnp.maximum(jnp.max(old, axis=1, keepdims=True), jnp.max(new, axis=1, keepdims=True))
            old = jnp.exp(old - top)
            new = jnp.exp(new - top)
            total = jnp.sum(old, axis=1, keepdims=True) + jnp.sum(new, axis=1, keepdims=True)
            mixed = dot(old.astype(BF16), old_v) + dot(new.astype(BF16), new_v)
            att[rows, columns] = mixed / total
        return carry

    lax.fori_loop(0, HEADS, attend, 0)

    for copy in every[1]:
        copy.wait_recv()
    total = eq[...] + erx[1, 0].astype(F32) + erx[1, 1].astype(F32) + erx[1, 2].astype(F32)
    gfull[2, my_quarter, :] = total.astype(BF16)
    for copy in every[2]:
        copy.start()

    owned = (2 * x + 1, 2 * y + 2)
    second_copies = [
        [
            remote(
                gs2.at[slot], rx2.at[slot, d - 1], ss2.at[slot, d - 1], rs2.at[slot, d - 1],
                on_axis(1 - slot, lax.rem(where[1 - slot] + d, 4)),
            )
            for d in (2, 1, 3)
        ]
        for slot in range(2)
    ]
    third_copies = [
        [
            remote(
                oall.at[owned[slot], mine], oall.at[owned[slot], mine], ss3.at[slot, d - 1], rs3.at[owned[slot]],
                on_axis(slot, lax.rem(where[slot] + d, 4)),
            )
            for d in (2, 1, 3)
        ]
        for slot in range(2)
    ]
    half_copies = [
        remote(gfull.at[slot, mine], gfull.at[slot, mine], ssx.at[slot], rsx.at[slot], sibling) for slot in range(3)
    ]

    for slot in range(2):
        m = owned[slot]
        total = gown[m]
        for d in range(3):
            remote(gs1.at[m], rx1.at[slot, d], ss1.at[m], rs1.at[slot, d], sibling).wait_recv()
            total = total + rx1[slot, d].astype(F32)
        gown[m] = total
        gs2[slot] = total.astype(BF16)
        for copy in second_copies[slot]:
            copy.start()

    for d, x_there in ((d, lax.rem(x + 4 - d, 4)) for d in (2, 1, 3)):
        theirs = quarter(c * 4 + x_there)
        remote(gfull.at[2, theirs], gfull.at[2, theirs], ess.at[2, d - 1], ers.at[2, d - 1], sibling).wait_recv()
    half_copies[2].start()

    for slot in range(2):
        total = gown[owned[slot]]
        for copy in second_copies[slot]:
            copy.wait_recv()
        for d in range(3):
            total = total + rx2[slot, d].astype(F32)
        gfull[slot, mine, :] = total.astype(BF16)
        half_copies[slot].start()

    for copy in half_copies:
        copy.wait_recv()

    iterates = []
    for slot in range(3):
        full = gfull[slot].astype(F32)
        norm = jnp.sqrt(jnp.sum(full * full, keepdims=True)) + EPS_SCALE
        iterates.append((full / norm).astype(BF16))
    for repeat in range(STEPS):
        grams = [dot_nt(it, it).astype(BF16) for it in iterates]
        mixing = [
            (COEF_B * gram.astype(F32) + COEF_C * dot(gram, gram)).astype(BF16) for gram in grams
        ]
        iterates = [
            (COEF_A * it.astype(F32) + dot(mix, it)).astype(BF16) for mix, it in zip(mixing, iterates)
        ]

    for slot in range(2):
        oall[owned[slot]] = iterates[slot]
    for pair in zip(*third_copies):
        for copy in pair:
            copy.start()
    oall[0] = iterates[2]

    fourth_copies = [
        remote(oall.at[m, mine], oall.at[m, mine], ss4.at[m], rs4.at[m], sibling) for m in range(MATS)
    ]

    def foreign(m, action):
        if m > 0:
            axis, place = PLACE[m]
            pl.when(where[axis] != place)(action)

    def forward(m):
        def action():
            remote(oall.at[m, mine], oall.at[m, mine], ss4.at[m], rs3.at[m], sibling).wait_recv()
            fourth_copies[m].start()

        foreign(m, action)

    def apply(h):
        for j in range(3):
            foreign(3 * h + j, fourth_copies[3 * h + j].wait_recv)
        columns = pl.ds(h * HDIM, HDIM)
        size = scale_ref[h]
        first = (w1[h] - size * oall[3 * h].astype(F32)).astype(BF16)
        third = (w3[h] - size * oall[3 * h + 1].astype(F32)).astype(BF16)
        second = (w2[h] - size * oall[3 * h + 2].astype(F32).T).astype(BF16)
        gain = gain_ref[pl.ds(h * HDIM, HDIM)].reshape(1, HDIM)
        for part in range(2):
            rows = pl.ds(part * HDIM, HDIM)
            queries = q[rows, columns]
            gate = dot(queries, first)
            up = dot(queries, third)
            hidden = (gate * jax.nn.sigmoid(gate) * up).astype(BF16)
            fast = dot(hidden, second)
            spread = jnp.mean(fast * fast, axis=1, keepdims=True)
            normed = fast * lax.rsqrt(spread + EPS_RMS) * gain
            out_ref[rows, columns] = (att[rows, columns] + normed).astype(BF16)

    for m in range(1, MATS):
        forward(m)
    for h in range(HEADS):
        apply(h)

    for copy in logit_copies + s0:
        copy.wait_send()

    @pl.when(tok < 31)
    def _():
        for copy in halo:
            copy.wait_send()

    for m in range(1, MATS):
        foreign(m, s1[m].wait_send)
        foreign(m, fourth_copies[m].wait_send)
    for copies in every + second_copies + [half_copies] + third_copies:
        for copy in copies:
            copy.wait_send()


def on_device(x, rw, q, k, v, w1, w3, w2, scale, gain):
    anywhere = pl.BlockSpec(memory_space=pl.ANY)
    dma = pltpu.SemaphoreType.DMA
    features = x.shape[1]
    wide = HEADS * HDIM
    return pl.pallas_call(
        kernel,
        name="layer",
        out_shape=jax.ShapeDtypeStruct((ROWS, wide), BF16),
        in_specs=[anywhere] * 8
        + [pl.BlockSpec(memory_space=pltpu.SMEM), pl.BlockSpec(memory_space=pltpu.VMEM)],
        out_specs=pl.BlockSpec(memory_space=pltpu.VMEM),
        scratch_shapes=[
            pltpu.VMEM((ROWS, features), BF16),
            pltpu.VMEM((rw.shape[1], rw.shape[0]), BF16),
            pltpu.VMEM((ROWS, wide), BF16),
            pltpu.VMEM((ROWS, wide), BF16),
            pltpu.VMEM((ROWS, wide), BF16),
            pltpu.VMEM((HEADS, HDIM, FFN), F32),
            pltpu.VMEM((HEADS, HDIM, FFN), F32),
            pltpu.VMEM((HEADS, FFN, HDIM), F32),
            dma((8,)),
            pltpu.VMEM((ROWS, 128), F32),
            pltpu.VMEM((4, 8, ROWS), F32),
            pltpu.VMEM((3, 8, ROWS), F32),
            dma((3,)),
            dma((3,)),
            pltpu.VMEM((HDIM, wide), BF16),
            pltpu.VMEM((HDIM, wide), BF16),
            dma((2,)),
            dma((2,)),
            pltpu.VMEM((HEADS, ROWS, FFN), F32),
            pltpu.VMEM((HEADS, ROWS, FFN), F32),
            pltpu.VMEM((HEADS, ROWS, FFN), F32),
            pltpu.VMEM((HEADS, HDIM, ROWS), BF16),
            pltpu.VMEM((HEADS, HDIM, ROWS), BF16),
            pltpu.VMEM((ROWS, wide), F32),
            pltpu.VMEM((QUARTER, FFN), F32),
            pltpu.VMEM((QUARTER, FFN), BF16),
            pltpu.VMEM((2, 3, QUARTER, FFN), BF16),
            dma((3, 3)),
            dma((3, 3)),
            pltpu.VMEM((MATS, HALF, FFN), F32),
            pltpu.VMEM((MATS, HALF, FFN), BF16),
            pltpu.VMEM((MATS, HALF, FFN), BF16),
            pltpu.VMEM((MATS, HALF, FFN), BF16),
            pltpu.VMEM((2, 3, HALF, FFN), BF16),
            pltpu.VMEM((2, HALF, FFN), BF16),
            pltpu.VMEM((2, 3, HALF, FFN), BF16),
            pltpu.VMEM((3, HDIM, FFN), BF16),
            pltpu.VMEM((MATS, HDIM, FFN), BF16),
            dma((MATS,)),
            dma((MATS,)),
            dma((MATS,)),
            dma((2, 3)),
            dma((2, 3)),
            dma((2, 3)),
            dma((3,)),
            dma((3,)),
            dma((2, 3)),
            dma((MATS,)),
            dma((MATS,)),
            dma((MATS,)),
        ],
        compiler_params=pltpu.CompilerParams(
            collective_id=0, has_side_effects=True, vmem_limit_bytes=56 << 20
        ),
    )(x, rw.T, q, k, v, w1, w3, w2, scale, gain)


def solution(mesh):
    placed = (
        P("tok", "head"),
        P("head", None),
        P("tok", "head"),
        P("tok", "head"),
        P("tok", "head"),
        P("head", None, None),
        P("head", None, None),
        P("head", None, None),
        P("head"),
        P("head"),
    )
    return jax.shard_map(
        on_device, mesh=mesh, in_specs=placed, out_specs=P("tok", "head"), check_vma=False
    )
```

```python
import jax
import jax.numpy as jnp
from jax import lax
from jax.experimental import pallas as pl
from jax.experimental.pallas import tpu as pltpu
from jax.sharding import PartitionSpec as P

MESH = pl.DeviceIdType.MESH
HDIM = 256
FFN = 512
HALF = 128
ROWS = 512
HEADS = 3
MATS = 9
STEPS = 5
COEF_A = 3.4445
COEF_B = -4.775
COEF_C = 2.0315
EPS_SCALE = 1e-07
EPS_RMS = 1e-06
F32 = jnp.float32
BF16 = jnp.bfloat16

PLACE = [None] + [((m - 1) % 2, (m - 1) // 2) for m in range(1, MATS)]
QUARTER = HALF // 4
LAG = 5


def dot(a, b):
    return jnp.dot(a, b, preferred_element_type=F32)


def dot_nt(a, b):
    return lax.dot_general(a, b, (((1,), (1,)), ((), ())), preferred_element_type=F32)


def kernel(
    x_hbm, rw_hbm, q_hbm, k_hbm, v_hbm, w1_hbm, w3_hbm, w2_hbm, scale_ref, gain_ref, out_ref,
    xin, rw, q, k, v, w1, w3, w2, load_sem,
    lpad, lg, lrx, lss, lrs,
    hk, hv, hss, hrs,
    pg, pu, hd, kt, vt, att, whole,
    eq, es, erx, ess, ers,
    gown, gs0, rx0, gs1, rx1, gs2, rx2, gfull, oall,
    ss0, rs0, ss1, rs1, ss2, rs2, ssx, rsx, ss3, rs3, ss4, rs4,
):
    tok = lax.axis_index("tok")
    z = lax.axis_index("head")
    c = lax.rem(tok, 2)
    x = lax.rem(lax.div(tok, 2), 4)
    y = lax.div(tok, 8)
    where = (x, y)

    def on_axis(axis, place):
        if axis == 0:
            return ((y * 4 + place) * 2 + c, z)
        return ((place * 4 + x) * 2 + c, z)

    sibling = (tok + 1 - 2 * c, z)

    def remote(src, dst, send, recv, device):
        return pltpu.make_async_remote_copy(
            src_ref=src, dst_ref=dst, send_sem=send, recv_sem=recv, device_id=device, device_id_type=MESH
        )

    def load(source, target, number):
        copy = pltpu.make_async_copy(source, target, load_sem.at[number])
        copy.start()
        return copy

    load_x = load(x_hbm, xin, 0)
    load_rw = load(rw_hbm, rw, 1)
    load_kv = [load(k_hbm, k, 2), load(v_hbm, v, 3)]
    load_w = [
        [load(a.at[h], b.at[h], 4 + 3 * h + i) for i, (a, b) in enumerate(((w1_hbm, w1), (w3_hbm, w3), (w2_hbm, w2)))]
        for h in range(HEADS)
    ]
    load_q = load(q_hbm, q, 13)

    barrier = pltpu.get_barrier_semaphore()

    def greet(device):
        pl.semaphore_signal(barrier, inc=1, device_id=device, device_id_type=MESH)

    greet(sibling)
    for d in range(1, 4):
        greet(on_axis(0, lax.rem(x + d, 4)))
        greet(on_axis(1, lax.rem(y + d, 4)))
        greet((tok, lax.rem(z + d, 4)))

    greet((lax.rem(tok + 31, 32), z))
    greet((lax.rem(tok + 1, 32), z))

    lpad[...] = jnp.zeros_like(lpad)
    lg[...] = jnp.zeros_like(lg)
    load_x.wait()
    load_rw.wait()
    lpad[:, 0:12] = dot_nt(xin[...], rw[...])
    turned = lpad[...].T
    for head in range(4):
        lg[head, 0:HEADS, :] = turned[HEADS * head : HEADS * (head + 1)]
    pl.semaphore_wait(barrier, 12)

    logit_copies = []
    for d in range(1, 4):
        there = lax.rem(z + d, 4)
        copy = remote(lg.at[there], lrx.at[d - 1], lss.at[d - 1], lrs.at[d - 1], (tok, there))
        copy.start()
        logit_copies.append(copy)

    for copy in load_kv:
        copy.wait()
    halo = [
        remote(k.at[pl.ds(ROWS - HDIM, HDIM)], hk, hss.at[0], hrs.at[0], (tok + 1, z)),
        remote(v.at[pl.ds(ROWS - HDIM, HDIM)], hv, hss.at[1], hrs.at[1], (tok + 1, z)),
    ]

    @pl.when(tok < 31)
    def _():
        for copy in halo:
            copy.start()

    @pl.when(tok == 0)
    def _():
        hk[...] = jnp.zeros_like(hk)
        hv[...] = jnp.zeros_like(hv)

    def before_rates(h):
        for copy in load_w[h]:
            copy.wait()
        columns = pl.ds(h * HDIM, HDIM)
        first = w1[h].astype(BF16)
        third = w3[h].astype(BF16)
        second = w2[h].astype(BF16)
        for part in range(2):
            rows = pl.ds(part * HDIM, HDIM)
            keys = k[rows, columns]
            values = v[rows, columns]
            kt[h, :, rows] = keys.T
            vt[h, :, rows] = values.T
            gate = dot(keys, first)
            up = dot(keys, third)
            back = -dot_nt(values, second)
            sig = jax.nn.sigmoid(gate)
            activ = gate * sig
            pg[h, rows, :] = back * up * sig * (1.0 + gate * (1.0 - sig))
            pu[h, rows, :] = back * activ
            hd[h, rows, :] = -(activ * up)

    for h in range(HEADS):
        before_rates(h)

    for copy in logit_copies:
        copy.wait_recv()
    logits = lg[z] + lrx[0] + lrx[1] + lrx[2]
    rates = jnp.maximum(logits, 0.0) + jnp.log1p(jnp.exp(-jnp.abs(logits)))
    rates_down = rates.T

    mine = pl.ds(pl.multiple_of(c * HALF, HALF), HALF)
    other = pl.ds(pl.multiple_of(HALF - c * HALF, HALF), HALF)

    s0 = [
        remote(gs0.at[m], rx0.at[m], ss0.at[m], rs0.at[m], sibling) for m in range(MATS)
    ]
    s1 = [None]
    for m in range(1, MATS):
        axis, place = PLACE[m]
        step = lax.rem(place - where[axis] + 4, 4)
        index = jnp.maximum(step - 1, 0)
        s1.append(
            remote(gs1.at[m], rx1.at[axis, index], ss1.at[m], rs1.at[axis, index], on_axis(axis, place))
        )

    def quarter(place):
        return pl.ds(pl.multiple_of(place * QUARTER, QUARTER), QUARTER)

    my_quarter = quarter(c * 4 + x)
    every = [[], [], []]
    for d in (2, 1, 3):
        x_there, y_there = lax.rem(x + d, 4), lax.rem(y + d, 4)
        every[0].append(
            remote(gs1.at[0, quarter(x_there)], erx.at[0, d - 1], ess.at[0, d - 1], ers.at[0, d - 1], on_axis(0, x_there))
        )
        every[1].append(remote(es, erx.at[1, d - 1], ess.at[1, d - 1], ers.at[1, d - 1], on_axis(1, y_there)))
        every[2].append(
            remote(
                gfull.at[2, my_quarter], gfull.at[2, my_quarter], ess.at[2, d - 1], ers.at[2, d - 1], on_axis(0, x_there)
            )
        )

    def send_chip_sum(m):
        s0[m].wait_recv()
        both = gown[m] + rx0[m].astype(F32)
        gown[m] = both
        gs1[m] = both.astype(BF16)
        if m == 0:
            for copy in every[0]:
                copy.start()
            return
        axis, place = PLACE[m]

        @pl.when(where[axis] != place)
        def _():
            s1[m].start()

    for h in range(HEADS):
        rate = rates_down[:, h : h + 1]
        wides = ((kt, pg), (kt, pu), (vt, hd))
        for j, (left, right) in enumerate(wides):
            m = 3 * h + j
            scaled = (rate * right[h]).astype(BF16)
            whole[m % 2] = dot(left[h], scaled)
            gs0[m] = whole[m % 2, other, :].astype(BF16)
            s0[m].start()
            gown[m] = whole[m % 2, mine, :]
            if m >= LAG:
                send_chip_sum(m - LAG)
    for m in range(MATS - LAG, MATS):
        send_chip_sum(m)
    for copy in every[0]:
        copy.wait_recv()
    total = gown[0, quarter(x), :]
    for d in range(3):
        total = total + erx[0, d].astype(F32)
    eq[...] = total
    es[...] = total.astype(BF16)
    for copy in every[1]:
        copy.start()

    load_q.wait()

    @pl.when(tok > 0)
    def _():
        for copy in halo:
            copy.wait_recv()

    row = lax.broadcasted_iota(jnp.int32, (HDIM, HDIM), 0)
    column = lax.broadcasted_iota(jnp.int32, (HDIM, HDIM), 1)
    has_past = tok > 0

    def attend(h, carry):
        columns = pl.ds(pl.multiple_of(h * HDIM, HDIM), HDIM)
        low, high = pl.ds(0, HDIM), pl.ds(HDIM, HDIM)
        blocks = (
            (low, hk[:, columns], hv[:, columns], k[low, columns], v[low, columns], True),
            (high, k[low, columns], v[low, columns], k[high, columns], v[high, columns], False),
        )
        for rows, old_k, old_v, new_k, new_v, edge in blocks:
            queries = q[rows, columns]
            seen = column > row
            if edge:
                seen = jnp.logical_and(seen, has_past)
            old = jnp.where(seen, dot_nt(queries, old_k) * HDIM ** (-0.5), -1e30)
            new = jnp.where(column <= row, dot_nt(queries, new_k) * HDIM ** (-0.5), -1e30)
            top = jnp.maximum(jnp.max(old, axis=1, keepdims=True), jnp.max(new, axis=1, keepdims=True))
            old = jnp.exp(old - top)
            new = jnp.exp(new - top)
            total = jnp.sum(old, axis=1, keepdims=True) + jnp.sum(new, axis=1, keepdims=True)
            mixed = dot(old.astype(BF16), old_v) + dot(new.astype(BF16), new_v)
            att[rows, columns] = mixed / total
        return carry

    lax.fori_loop(0, HEADS, attend, 0)

    owned = (2 * x + 1, 2 * y + 2)
    second_copies = [
        [
            remote(
                gs2.at[slot], rx2.at[slot, d - 1], ss2.at[slot, d - 1], rs2.at[slot, d - 1],
                on_axis(1 - slot, lax.rem(where[1 - slot] + d, 4)),
            )
            for d in (2, 1, 3)
        ]
        for slot in range(2)
    ]
    third_copies = [
        [
            remote(
                oall.at[owned[slot], mine], oall.at[owned[slot], mine], ss3.at[slot, d - 1], rs3.at[owned[slot]],
                on_axis(slot, lax.rem(where[slot] + d, 4)),
            )
            for d in (2, 1, 3)
        ]
        for slot in range(2)
    ]
    half_copies = [
        remote(gfull.at[slot, mine], gfull.at[slot, mine], ssx.at[slot], rsx.at[slot], sibling) for slot in range(3)
    ]

    def first_sum(slot):
        m = owned[slot]
        total = gown[m]
        for d in range(3):
            remote(gs1.at[m], rx1.at[slot, d], ss1.at[m], rs1.at[slot, d], sibling).wait_recv()
            total = total + rx1[slot, d].astype(F32)
        gown[m] = total
        gs2[slot] = total.astype(BF16)
        for copy in second_copies[slot]:
            copy.start()

    def second_sum(slot):
        total = gown[owned[slot]]
        for copy in second_copies[slot]:
            copy.wait_recv()
        for d in range(3):
            total = total + rx2[slot, d].astype(F32)
        gfull[slot, mine, :] = total.astype(BF16)
        half_copies[slot].start()

    def orthogonalize(slots):
        iterates = []
        for slot in slots:
            half_copies[slot].wait_recv()
            full = gfull[slot].astype(F32)
            norm = jnp.sqrt(jnp.sum(full * full, keepdims=True)) + EPS_SCALE
            iterates.append((full / norm).astype(BF16))
        for repeat in range(STEPS):
            grams = [dot_nt(it, it).astype(BF16) for it in iterates]
            mixing = [
                (COEF_B * gram.astype(F32) + COEF_C * dot(gram, gram)).astype(BF16) for gram in grams
            ]
            iterates = [
                (COEF_A * it.astype(F32) + dot(mix, it)).astype(BF16) for mix, it in zip(mixing, iterates)
            ]
        for slot, it in zip(slots, iterates):
            oall[0 if slot == 2 else owned[slot]] = it

    first_sum(0)
    first_sum(1)
    for copy in every[1]:
        copy.wait_recv()
    total = eq[...]
    for d in range(3):
        total = total + erx[1, d].astype(F32)
    gfull[2, my_quarter, :] = total.astype(BF16)
    for copy in every[2]:
        copy.start()
    second_sum(0)
    second_sum(1)
    orthogonalize([0, 1])
    for pair in zip(*third_copies):
        for copy in pair:
            copy.start()
    for d in (2, 1, 3):
        theirs = quarter(c * 4 + lax.rem(x + 4 - d, 4))
        remote(gfull.at[2, theirs], gfull.at[2, theirs], ess.at[2, d - 1], ers.at[2, d - 1], sibling).wait_recv()
    half_copies[2].start()
    orthogonalize([2])

    fourth_copies = [None] + [
        remote(oall.at[m, mine], oall.at[m, mine], ss4.at[m], rs4.at[m], sibling) for m in range(1, MATS)
    ]

    def foreign(m, action):
        axis, place = PLACE[m]
        pl.when(where[axis] != place)(action)

    def forward(d):
        for m in (2 * lax.rem(x + d, 4) + 1, 2 * lax.rem(y + d, 4) + 2):
            part = oall.at[m, mine]
            remote(part, part, ss4.at[m], rs3.at[m], sibling).wait_recv()
            remote(part, part, ss4.at[m], rs4.at[m], sibling).start()

    def apply(h):
        for j in range(3):
            if 3 * h + j > 0:
                foreign(3 * h + j, fourth_copies[3 * h + j].wait_recv)
        columns = pl.ds(h * HDIM, HDIM)
        size = scale_ref[h]
        first = (w1[h] - size * oall[3 * h].astype(F32)).astype(BF16)
        third = (w3[h] - size * oall[3 * h + 1].astype(F32)).astype(BF16)
        second = (w2[h] - size * oall[3 * h + 2].astype(F32).T).astype(BF16)
        gain = gain_ref[pl.ds(h * HDIM, HDIM)].reshape(1, HDIM)
        for part in range(2):
            rows = pl.ds(part * HDIM, HDIM)
            queries = q[rows, columns]
            gate = dot(queries, first)
            up = dot(queries, third)
            hidden = (gate * jax.nn.sigmoid(gate) * up).astype(BF16)
            fast = dot(hidden, second)
            spread = jnp.mean(fast * fast, axis=1, keepdims=True)
            normed = fast * lax.rsqrt(spread + EPS_RMS) * gain
            out_ref[rows, columns] = (att[rows, columns] + normed).astype(BF16)

    for d in (1, 3, 2):
        forward(d)
    for h in range(HEADS):
        apply(h)

    for copy in logit_copies + s0:
        copy.wait_send()

    @pl.when(tok < 31)
    def _():
        for copy in halo:
            copy.wait_send()

    for m in range(1, MATS):
        foreign(m, s1[m].wait_send)
        foreign(m, fourth_copies[m].wait_send)
    for copies in every + second_copies + [half_copies] + third_copies:
        for copy in copies:
            copy.wait_send()


def on_device(x, rw, q, k, v, w1, w3, w2, scale, gain):
    anywhere = pl.BlockSpec(memory_space=pl.ANY)
    dma = pltpu.SemaphoreType.DMA
    features = x.shape[1]
    wide = HEADS * HDIM
    return pl.pallas_call(
        kernel,
        name="layer",
        out_shape=jax.ShapeDtypeStruct((ROWS, wide), BF16),
        in_specs=[anywhere] * 8
        + [pl.BlockSpec(memory_space=pltpu.SMEM), pl.BlockSpec(memory_space=pltpu.VMEM)],
        out_specs=pl.BlockSpec(memory_space=pltpu.VMEM),
        scratch_shapes=[
            pltpu.VMEM((ROWS, features), BF16),
            pltpu.VMEM((rw.shape[1], rw.shape[0]), BF16),
            pltpu.VMEM((ROWS, wide), BF16),
            pltpu.VMEM((ROWS, wide), BF16),
            pltpu.VMEM((ROWS, wide), BF16),
            pltpu.VMEM((HEADS, HDIM, FFN), F32),
            pltpu.VMEM((HEADS, HDIM, FFN), F32),
            pltpu.VMEM((HEADS, FFN, HDIM), F32),
            dma((14,)),
            pltpu.VMEM((ROWS, 128), F32),
            pltpu.VMEM((4, 8, ROWS), F32),
            pltpu.VMEM((3, 8, ROWS), F32),
            dma((3,)),
            dma((3,)),
            pltpu.VMEM((HDIM, wide), BF16),
            pltpu.VMEM((HDIM, wide), BF16),
            dma((2,)),
            dma((2,)),
            pltpu.VMEM((HEADS, ROWS, FFN), F32),
            pltpu.VMEM((HEADS, ROWS, FFN), F32),
            pltpu.VMEM((HEADS, ROWS, FFN), F32),
            pltpu.VMEM((HEADS, HDIM, ROWS), BF16),
            pltpu.VMEM((HEADS, HDIM, ROWS), BF16),
            pltpu.VMEM((ROWS, wide), F32),
            pltpu.VMEM((2, HDIM, FFN), F32),
            pltpu.VMEM((QUARTER, FFN), F32),
            pltpu.VMEM((QUARTER, FFN), BF16),
            pltpu.VMEM((2, 3, QUARTER, FFN), BF16),
            dma((3, 3)),
            dma((3, 3)),
            pltpu.VMEM((MATS, HALF, FFN), F32),
            pltpu.VMEM((MATS, HALF, FFN), BF16),
            pltpu.VMEM((MATS, HALF, FFN), BF16),
            pltpu.VMEM((MATS, HALF, FFN), BF16),
            pltpu.VMEM((2, 3, HALF, FFN), BF16),
            pltpu.VMEM((2, HALF, FFN), BF16),
            pltpu.VMEM((2, 3, HALF, FFN), BF16),
            pltpu.VMEM((3, HDIM, FFN), BF16),
            pltpu.VMEM((MATS, HDIM, FFN), BF16),
            dma((MATS,)),
            dma((MATS,)),
            dma((MATS,)),
            dma((2, 3)),
            dma((2, 3)),
            dma((2, 3)),
            dma((3,)),
            dma((3,)),
            dma((2, 3)),
            dma((MATS,)),
            dma((MATS,)),
            dma((MATS,)),
        ],
        compiler_params=pltpu.CompilerParams(
            collective_id=0, has_side_effects=True, vmem_limit_bytes=56 << 20
        ),
    )(x, rw.T, q, k, v, w1, w3, w2, scale, gain)


def solution(mesh):
    placed = (
        P("tok", "head"),
        P("head", None),
        P("tok", "head"),
        P("tok", "head"),
        P("tok", "head"),
        P("head", None, None),
        P("head", None, None),
        P("head", None, None),
        P("head"),
        P("head"),
    )
    return jax.shard_map(
        on_device, mesh=mesh, in_specs=placed, out_specs=P("tok", "head"), check_vma=False
    )
```

```python
import jax
import jax.numpy as jnp
from jax import lax
from jax.experimental import pallas as pl
from jax.experimental.pallas import tpu as pltpu
from jax.sharding import PartitionSpec as P

MESH = pl.DeviceIdType.MESH
HDIM = 256
FFN = 512
HALF = 128
ROWS = 512
HEADS = 3
MATS = 9
STEPS = 5
COEF_A = 3.4445
COEF_B = -4.775
COEF_C = 2.0315
EPS_SCALE = 1e-07
EPS_RMS = 1e-06
F32 = jnp.float32
BF16 = jnp.bfloat16

PLACE = [None] + [((m - 1) % 2, (m - 1) // 2) for m in range(1, MATS)]
QUARTER = HALF // 4
LAG = 5
SPLIT = 2
PART = HALF // SPLIT
PARTS = [pl.ds(i * PART, PART) for i in range(SPLIT)]


def dot(a, b):
    return jnp.dot(a, b, preferred_element_type=F32)


def dot_nt(a, b):
    return lax.dot_general(a, b, (((1,), (1,)), ((), ())), preferred_element_type=F32)


def kernel(
    x_hbm, rw_hbm, q_hbm, k_hbm, v_hbm, w1_hbm, w3_hbm, w2_hbm, scale_ref, gain_ref, out_hbm,
    out_ref, out_sem,
    xin, rw, q, k, v, w1, w3, w2, load_sem,
    lpad, lg, lrx, lss, lrs,
    hk, hv, hss, hrs,
    pg, pu, hd, kt, vt, att, whole,
    eq, es, erx, ess, ers,
    gown, gs0, rx0, gs1, rx1, gs2, rx2, gfull, oall,
    ss0, rs0, ss1, rs1, ss2, rs2, ssx, rsx, ss3, rs3, ss4, rs4,
):
    tok = lax.axis_index("tok")
    z = lax.axis_index("head")
    c = lax.rem(tok, 2)
    x = lax.rem(lax.div(tok, 2), 4)
    y = lax.div(tok, 8)
    where = (x, y)

    def on_axis(axis, place):
        if axis == 0:
            return ((y * 4 + place) * 2 + c, z)
        return ((place * 4 + x) * 2 + c, z)

    sibling = (tok + 1 - 2 * c, z)

    def remote(src, dst, send, recv, device):
        return pltpu.make_async_remote_copy(
            src_ref=src, dst_ref=dst, send_sem=send, recv_sem=recv, device_id=device, device_id_type=MESH
        )

    def load(source, target, number):
        copy = pltpu.make_async_copy(source, target, load_sem.at[number])
        copy.start()
        return copy

    load_x = load(x_hbm, xin, 0)
    load_rw = load(rw_hbm, rw, 1)
    load_kv = [load(k_hbm, k, 2), load(v_hbm, v, 3)]
    load_w = [
        [load(a.at[h], b.at[h], 4 + 3 * h + i) for i, (a, b) in enumerate(((w1_hbm, w1), (w3_hbm, w3), (w2_hbm, w2)))]
        for h in range(HEADS)
    ]
    load_q = load(q_hbm, q, 13)

    barrier = pltpu.get_barrier_semaphore()

    def greet(device):
        pl.semaphore_signal(barrier, inc=1, device_id=device, device_id_type=MESH)

    greet(sibling)
    for d in range(1, 4):
        greet(on_axis(0, lax.rem(x + d, 4)))
        greet(on_axis(1, lax.rem(y + d, 4)))
        greet((tok, lax.rem(z + d, 4)))

    greet((lax.rem(tok + 31, 32), z))
    greet((lax.rem(tok + 1, 32), z))

    lpad[...] = jnp.zeros_like(lpad)
    lg[...] = jnp.zeros_like(lg)
    load_x.wait()
    load_rw.wait()
    lpad[:, 0:12] = dot_nt(xin[...], rw[...])
    turned = lpad[...].T
    for head in range(4):
        lg[head, 0:HEADS, :] = turned[HEADS * head : HEADS * (head + 1)]
    pl.semaphore_wait(barrier, 12)

    logit_copies = []
    for d in range(1, 4):
        there = lax.rem(z + d, 4)
        copy = remote(lg.at[there], lrx.at[d - 1], lss.at[d - 1], lrs.at[d - 1], (tok, there))
        copy.start()
        logit_copies.append(copy)

    for copy in load_kv:
        copy.wait()
    halo = [
        remote(k.at[pl.ds(ROWS - HDIM, HDIM)], hk, hss.at[0], hrs.at[0], (tok + 1, z)),
        remote(v.at[pl.ds(ROWS - HDIM, HDIM)], hv, hss.at[1], hrs.at[1], (tok + 1, z)),
    ]

    @pl.when(tok < 31)
    def _():
        for copy in halo:
            copy.start()

    @pl.when(tok == 0)
    def _():
        hk[...] = jnp.zeros_like(hk)
        hv[...] = jnp.zeros_like(hv)

    def before_rates(h):
        for copy in load_w[h]:
            copy.wait()
        columns = pl.ds(h * HDIM, HDIM)
        first = w1[h].astype(BF16)
        third = w3[h].astype(BF16)
        second = w2[h].astype(BF16)
        for part in range(2):
            rows = pl.ds(part * HDIM, HDIM)
            keys = k[rows, columns]
            values = v[rows, columns]
            kt[h, :, rows] = keys.T
            vt[h, :, rows] = values.T
            gate = dot(keys, first)
            up = dot(keys, third)
            back = -dot_nt(values, second)
            sig = jax.nn.sigmoid(gate)
            activ = gate * sig
            pg[h, rows, :] = back * up * sig * (1.0 + gate * (1.0 - sig))
            pu[h, rows, :] = back * activ
            hd[h, rows, :] = -(activ * up)

    for h in range(HEADS):
        before_rates(h)

    for copy in logit_copies:
        copy.wait_recv()
    logits = lg[z] + lrx[0] + lrx[1] + lrx[2]
    rates = jnp.maximum(logits, 0.0) + jnp.log1p(jnp.exp(-jnp.abs(logits)))
    rates_down = rates.T

    mine = pl.ds(pl.multiple_of(c * HALF, HALF), HALF)
    other = pl.ds(pl.multiple_of(HALF - c * HALF, HALF), HALF)

    s0 = [
        remote(gs0.at[m], rx0.at[m], ss0.at[m], rs0.at[m], sibling) for m in range(MATS)
    ]
    s1 = [None]
    for m in range(1, MATS):
        axis, place = PLACE[m]
        step = lax.rem(place - where[axis] + 4, 4)
        index = jnp.maximum(step - 1, 0)
        s1.append(
            [
                remote(
                    gs1.at[m, part], rx1.at[axis, index, part], ss1.at[m, i], rs1.at[axis, index, i],
                    on_axis(axis, place),
                )
                for i, part in enumerate(PARTS)
            ]
        )

    def quarter(place):
        return pl.ds(pl.multiple_of(place * QUARTER, QUARTER), QUARTER)

    my_quarter = quarter(c * 4 + x)
    every = [[], [], []]
    for d in (2, 1, 3):
        x_there, y_there = lax.rem(x + d, 4), lax.rem(y + d, 4)
        every[0].append(
            remote(gs1.at[0, quarter(x_there)], erx.at[0, d - 1], ess.at[0, d - 1], ers.at[0, d - 1], on_axis(0, x_there))
        )
        every[1].append(remote(es, erx.at[1, d - 1], ess.at[1, d - 1], ers.at[1, d - 1], on_axis(1, y_there)))
        every[2].append(
            remote(
                gfull.at[2, my_quarter], gfull.at[2, my_quarter], ess.at[2, d - 1], ers.at[2, d - 1], on_axis(0, x_there)
            )
        )

    def send_chip_sum(m):
        s0[m].wait_recv()
        both = gown[m] + rx0[m].astype(F32)
        gown[m] = both
        gs1[m] = both.astype(BF16)
        if m == 0:
            for copy in every[0]:
                copy.start()
            return
        axis, place = PLACE[m]

        @pl.when(where[axis] != place)
        def _():
            for copy in s1[m]:
                copy.start()

    for h in range(HEADS):
        rate = rates_down[:, h : h + 1]
        wides = ((kt, pg), (kt, pu), (vt, hd))
        for j, (left, right) in enumerate(wides):
            m = 3 * h + j
            scaled = (rate * right[h]).astype(BF16)
            whole[m % 2] = dot(left[h], scaled)
            gs0[m] = whole[m % 2, other, :].astype(BF16)
            s0[m].start()
            gown[m] = whole[m % 2, mine, :]
            if m >= LAG:
                send_chip_sum(m - LAG)
    for m in range(MATS - LAG, MATS):
        send_chip_sum(m)
    for copy in every[0]:
        copy.wait_recv()
    total = gown[0, quarter(x), :]
    for d in range(3):
        total = total + erx[0, d].astype(F32)
    eq[...] = total
    es[...] = total.astype(BF16)
    for copy in every[1]:
        copy.start()

    load_q.wait()

    @pl.when(tok > 0)
    def _():
        for copy in halo:
            copy.wait_recv()

    row = lax.broadcasted_iota(jnp.int32, (HDIM, HDIM), 0)
    column = lax.broadcasted_iota(jnp.int32, (HDIM, HDIM), 1)
    has_past = tok > 0

    def attend(h, carry):
        columns = pl.ds(pl.multiple_of(h * HDIM, HDIM), HDIM)
        low, high = pl.ds(0, HDIM), pl.ds(HDIM, HDIM)
        blocks = (
            (low, hk[:, columns], hv[:, columns], k[low, columns], v[low, columns], True),
            (high, k[low, columns], v[low, columns], k[high, columns], v[high, columns], False),
        )
        for rows, old_k, old_v, new_k, new_v, edge in blocks:
            queries = q[rows, columns]
            seen = column > row
            if edge:
                seen = jnp.logical_and(seen, has_past)
            old = jnp.where(seen, dot_nt(queries, old_k) * HDIM ** (-0.5), -1e30)
            new = jnp.where(column <= row, dot_nt(queries, new_k) * HDIM ** (-0.5), -1e30)
            top = jnp.maximum(jnp.max(old, axis=1, keepdims=True), jnp.max(new, axis=1, keepdims=True))
            old = jnp.exp(old - top)
            new = jnp.exp(new - top)
            total = jnp.sum(old, axis=1, keepdims=True) + jnp.sum(new, axis=1, keepdims=True)
            mixed = dot(old.astype(BF16), old_v) + dot(new.astype(BF16), new_v)
            att[rows, columns] = mixed / total
        return carry

    lax.fori_loop(0, HEADS, attend, 0)

    owned = (2 * x + 1, 2 * y + 2)
    second_copies = [
        [
            remote(
                gs2.at[slot, part], rx2.at[slot, d - 1, part], ss2.at[slot, d - 1, i], rs2.at[slot, d - 1, i],
                on_axis(1 - slot, lax.rem(where[1 - slot] + d, 4)),
            )
            for i, part in enumerate(PARTS)
            for d in (2, 1, 3)
        ]
        for slot in range(2)
    ]
    def my_part(i):
        return pl.ds(pl.multiple_of(c * HALF + i * PART, PART), PART)

    third_copies = [
        [
            remote(
                oall.at[owned[slot], my_part(i)], oall.at[owned[slot], my_part(i)],
                ss3.at[slot, d - 1, i], rs3.at[owned[slot], i], on_axis(slot, lax.rem(where[slot] + d, 4)),
            )
            for i in range(SPLIT)
            for d in (2, 1, 3)
        ]
        for slot in range(2)
    ]
    half_copies = [
        [
            remote(gfull.at[slot, my_part(i)], gfull.at[slot, my_part(i)], ssx.at[slot, i], rsx.at[slot, i], sibling)
            for i in range(SPLIT)
        ]
        for slot in range(2)
    ] + [[remote(gfull.at[2, mine], gfull.at[2, mine], ssx.at[2, 0], rsx.at[2, 0], sibling)]]

    def first_sum(slot, i):
        m, part = owned[slot], PARTS[i]
        total = gown[m, part, :]
        for d in range(3):
            remote(gs1.at[m, part], rx1.at[slot, d, part], ss1.at[m, i], rs1.at[slot, d, i], sibling).wait_recv()
            total = total + rx1[slot, d, part, :].astype(F32)
        gown[m, part, :] = total
        gs2[slot, part, :] = total.astype(BF16)
        for copy in second_copies[slot][3 * i : 3 * i + 3]:
            copy.start()

    def second_sum(slot, i):
        total = gown[owned[slot], PARTS[i], :]
        for copy in second_copies[slot][3 * i : 3 * i + 3]:
            copy.wait_recv()
        for d in range(3):
            total = total + rx2[slot, d, PARTS[i], :].astype(F32)
        gfull[slot, my_part(i), :] = total.astype(BF16)
        half_copies[slot][i].start()

    def orthogonalize(slots):
        iterates = []
        for slot in slots:
            for copy in half_copies[slot]:
                copy.wait_recv()
            full = gfull[slot].astype(F32)
            norm = jnp.sqrt(jnp.sum(full * full, keepdims=True)) + EPS_SCALE
            iterates.append((full / norm).astype(BF16))
        for repeat in range(STEPS):
            grams = [dot_nt(it, it).astype(BF16) for it in iterates]
            mixing = [
                (COEF_B * gram.astype(F32) + COEF_C * dot(gram, gram)).astype(BF16) for gram in grams
            ]
            iterates = [
                (COEF_A * it.astype(F32) + dot(mix, it)).astype(BF16) for mix, it in zip(mixing, iterates)
            ]
        for slot, it in zip(slots, iterates):
            oall[0 if slot == 2 else owned[slot]] = it

    for i in range(SPLIT):
        first_sum(0, i)
        first_sum(1, i)
    for copy in every[1]:
        copy.wait_recv()
    total = eq[...]
    for d in range(3):
        total = total + erx[1, d].astype(F32)
    gfull[2, my_quarter, :] = total.astype(BF16)
    for copy in every[2]:
        copy.start()
    for i in range(SPLIT):
        second_sum(0, i)
        second_sum(1, i)
    orthogonalize([0, 1])
    for pair in zip(*third_copies):
        for copy in pair:
            copy.start()
    for d in (2, 1, 3):
        theirs = quarter(c * 4 + lax.rem(x + 4 - d, 4))
        remote(gfull.at[2, theirs], gfull.at[2, theirs], ess.at[2, d - 1], ers.at[2, d - 1], sibling).wait_recv()
    half_copies[2][0].start()
    orthogonalize([2])

    fourth_copies = [None] + [
        [
            remote(oall.at[m, my_part(i)], oall.at[m, my_part(i)], ss4.at[m, i], rs4.at[m, i], sibling)
            for i in range(SPLIT)
        ]
        for m in range(1, MATS)
    ]

    def foreign(m, action):
        axis, place = PLACE[m]
        pl.when(where[axis] != place)(action)

    def forward(d, i):
        for m in (2 * lax.rem(x + d, 4) + 1, 2 * lax.rem(y + d, 4) + 2):
            part = oall.at[m, my_part(i)]
            remote(part, part, ss4.at[m, i], rs3.at[m, i], sibling).wait_recv()
            remote(part, part, ss4.at[m, i], rs4.at[m, i], sibling).start()

    def apply(h):
        for j in range(3):
            if 3 * h + j > 0:
                for copy in fourth_copies[3 * h + j]:
                    foreign(3 * h + j, copy.wait_recv)
        columns = pl.ds(h * HDIM, HDIM)
        size = scale_ref[h]
        first = (w1[h] - size * oall[3 * h].astype(F32)).astype(BF16)
        third = (w3[h] - size * oall[3 * h + 1].astype(F32)).astype(BF16)
        second = (w2[h] - size * oall[3 * h + 2].astype(F32).T).astype(BF16)
        gain = gain_ref[pl.ds(h * HDIM, HDIM)].reshape(1, HDIM)
        for part in range(2):
            rows = pl.ds(part * HDIM, HDIM)
            queries = q[rows, columns]
            gate = dot(queries, first)
            up = dot(queries, third)
            hidden = (gate * jax.nn.sigmoid(gate) * up).astype(BF16)
            fast = dot(hidden, second)
            spread = jnp.mean(fast * fast, axis=1, keepdims=True)
            normed = fast * lax.rsqrt(spread + EPS_RMS) * gain
            out_ref[rows, columns] = (att[rows, columns] + normed).astype(BF16)

    for i in range(SPLIT):
        for d in (1, 3, 2):
            forward(d, i)
    out_copies = []
    for h in range(HEADS):
        apply(h)
        columns = pl.ds(h * HDIM, HDIM)
        copy = pltpu.make_async_copy(out_ref.at[:, columns], out_hbm.at[:, columns], out_sem.at[h])
        copy.start()
        out_copies.append(copy)

    for copy in out_copies:
        copy.wait()
    for copy in logit_copies + s0:
        copy.wait_send()

    @pl.when(tok < 31)
    def _():
        for copy in halo:
            copy.wait_send()

    for m in range(1, MATS):
        for copy in s1[m] + fourth_copies[m]:
            foreign(m, copy.wait_send)
    for copies in every + second_copies + half_copies + third_copies:
        for copy in copies:
            copy.wait_send()


def on_device(x, rw, q, k, v, w1, w3, w2, scale, gain):
    anywhere = pl.BlockSpec(memory_space=pl.ANY)
    dma = pltpu.SemaphoreType.DMA
    features = x.shape[1]
    wide = HEADS * HDIM
    return pl.pallas_call(
        kernel,
        name="layer",
        out_shape=jax.ShapeDtypeStruct((ROWS, wide), BF16),
        in_specs=[anywhere] * 8
        + [pl.BlockSpec(memory_space=pltpu.SMEM), pl.BlockSpec(memory_space=pltpu.VMEM)],
        out_specs=anywhere,
        scratch_shapes=[
            pltpu.VMEM((ROWS, wide), BF16),
            dma((HEADS,)),
            pltpu.VMEM((ROWS, features), BF16),
            pltpu.VMEM((rw.shape[1], rw.shape[0]), BF16),
            pltpu.VMEM((ROWS, wide), BF16),
            pltpu.VMEM((ROWS, wide), BF16),
            pltpu.VMEM((ROWS, wide), BF16),
            pltpu.VMEM((HEADS, HDIM, FFN), F32),
            pltpu.VMEM((HEADS, HDIM, FFN), F32),
            pltpu.VMEM((HEADS, FFN, HDIM), F32),
            dma((14,)),
            pltpu.VMEM((ROWS, 128), F32),
            pltpu.VMEM((4, 8, ROWS), F32),
            pltpu.VMEM((3, 8, ROWS), F32),
            dma((3,)),
            dma((3,)),
            pltpu.VMEM((HDIM, wide), BF16),
            pltpu.VMEM((HDIM, wide), BF16),
            dma((2,)),
            dma((2,)),
            pltpu.VMEM((HEADS, ROWS, FFN), F32),
            pltpu.VMEM((HEADS, ROWS, FFN), F32),
            pltpu.VMEM((HEADS, ROWS, FFN), F32),
            pltpu.VMEM((HEADS, HDIM, ROWS), BF16),
            pltpu.VMEM((HEADS, HDIM, ROWS), BF16),
            pltpu.VMEM((ROWS, wide), F32),
            pltpu.VMEM((2, HDIM, FFN), F32),
            pltpu.VMEM((QUARTER, FFN), F32),
            pltpu.VMEM((QUARTER, FFN), BF16),
            pltpu.VMEM((2, 3, QUARTER, FFN), BF16),
            dma((3, 3)),
            dma((3, 3)),
            pltpu.VMEM((MATS, HALF, FFN), F32),
            pltpu.VMEM((MATS, HALF, FFN), BF16),
            pltpu.VMEM((MATS, HALF, FFN), BF16),
            pltpu.VMEM((MATS, HALF, FFN), BF16),
            pltpu.VMEM((2, 3, HALF, FFN), BF16),
            pltpu.VMEM((2, HALF, FFN), BF16),
            pltpu.VMEM((2, 3, HALF, FFN), BF16),
            pltpu.VMEM((3, HDIM, FFN), BF16),
            pltpu.VMEM((MATS, HDIM, FFN), BF16),
            dma((MATS,)),
            dma((MATS,)),
            dma((MATS, SPLIT)),
            dma((2, 3, SPLIT)),
            dma((2, 3, SPLIT)),
            dma((2, 3, SPLIT)),
            dma((3, SPLIT)),
            dma((3, SPLIT)),
            dma((2, 3, SPLIT)),
            dma((MATS, SPLIT)),
            dma((MATS, SPLIT)),
            dma((MATS, SPLIT)),
        ],
        compiler_params=pltpu.CompilerParams(
            collective_id=0, has_side_effects=True, vmem_limit_bytes=56 << 20
        ),
    )(x, rw.T, q, k, v, w1, w3, w2, scale, gain)


def solution(mesh):
    placed = (
        P("tok", "head"),
        P("head", None),
        P("tok", "head"),
        P("tok", "head"),
        P("tok", "head"),
        P("head", None, None),
        P("head", None, None),
        P("head", None, None),
        P("head"),
        P("head"),
    )
    return jax.shard_map(
        on_device, mesh=mesh, in_specs=placed, out_specs=P("tok", "head"), check_vma=False
    )
```

```python
import jax
import jax.numpy as jnp
from jax import lax
from jax.experimental import pallas as pl
from jax.experimental.pallas import tpu as pltpu
from jax.sharding import PartitionSpec as P

MESH = pl.DeviceIdType.MESH
HDIM = 256
FFN = 512
HALF = 128
ROWS = 512
HEADS = 3
MATS = 9
STEPS = 5
COEF_A = 3.4445
COEF_B = -4.775
COEF_C = 2.0315
EPS_SCALE = 1e-07
EPS_RMS = 1e-06
F32 = jnp.float32
BF16 = jnp.bfloat16

PLACE = [None] + [((m - 1) % 2, (m - 1) // 2) for m in range(1, MATS)]
QUARTER = HALF // 4
LAG = 4
SPLIT = 2
PART = HALF // SPLIT
PARTS = [pl.ds(i * PART, PART) for i in range(SPLIT)]


def dot(a, b):
    return jnp.dot(a, b, preferred_element_type=F32)


def dot_nt(a, b):
    return lax.dot_general(a, b, (((1,), (1,)), ((), ())), preferred_element_type=F32)


def kernel(
    x_hbm, rw_hbm, q_hbm, k_hbm, v_hbm, w1_hbm, w3_hbm, w2_hbm, scale_ref, gain_ref, out_hbm,
    out_ref, out_sem,
    xin, rw, q, k, v, w1, w3, w2, load_sem,
    lpad, lg, lrx, lss, lrs,
    hk, hv, hss, hrs,
    pg, pu, hd, kt, vt, att, whole,
    eq, es, erx, ess, ers,
    gown, gs0, rx0, gs1, rx1, gs2, rx2, gfull, oall,
    ss0, rs0, ss1, rs1, ss2, rs2, ssx, rsx, ss3, rs3, ss4, rs4,
):
    tok = lax.axis_index("tok")
    z = lax.axis_index("head")
    c = lax.rem(tok, 2)
    x = lax.rem(lax.div(tok, 2), 4)
    y = lax.div(tok, 8)
    where = (x, y)

    def on_axis(axis, place):
        if axis == 0:
            return ((y * 4 + place) * 2 + c, z)
        return ((place * 4 + x) * 2 + c, z)

    sibling = (tok + 1 - 2 * c, z)

    def remote(src, dst, send, recv, device):
        return pltpu.make_async_remote_copy(
            src_ref=src, dst_ref=dst, send_sem=send, recv_sem=recv, device_id=device, device_id_type=MESH
        )

    def load(source, target, number):
        copy = pltpu.make_async_copy(source, target, load_sem.at[number])
        copy.start()
        return copy

    load_x = load(x_hbm, xin, 0)
    load_rw = load(rw_hbm, rw, 1)
    load_kv = [load(k_hbm, k, 2), load(v_hbm, v, 3)]
    load_w = [
        [load(a.at[h], b.at[h], 4 + 3 * h + i) for i, (a, b) in enumerate(((w1_hbm, w1), (w3_hbm, w3), (w2_hbm, w2)))]
        for h in range(HEADS)
    ]
    load_q = load(q_hbm, q, 13)

    barrier = pltpu.get_barrier_semaphore()

    def greet(device):
        pl.semaphore_signal(barrier, inc=1, device_id=device, device_id_type=MESH)

    greet(sibling)
    for d in range(1, 4):
        greet(on_axis(0, lax.rem(x + d, 4)))
        greet(on_axis(1, lax.rem(y + d, 4)))
        greet((tok, lax.rem(z + d, 4)))

    greet((lax.rem(tok + 31, 32), z))
    greet((lax.rem(tok + 1, 32), z))

    lpad[...] = jnp.zeros_like(lpad)
    lg[...] = jnp.zeros_like(lg)
    load_x.wait()
    load_rw.wait()
    lpad[:, 0:12] = dot_nt(xin[...], rw[...])
    turned = lpad[...].T
    for head in range(4):
        lg[head, 0:HEADS, :] = turned[HEADS * head : HEADS * (head + 1)]
    pl.semaphore_wait(barrier, 12)

    logit_copies = []
    for d in range(1, 4):
        there = lax.rem(z + d, 4)
        copy = remote(lg.at[there], lrx.at[d - 1], lss.at[d - 1], lrs.at[d - 1], (tok, there))
        copy.start()
        logit_copies.append(copy)

    for copy in load_kv:
        copy.wait()
    halo = [
        remote(k.at[pl.ds(ROWS - HDIM, HDIM)], hk, hss.at[0], hrs.at[0], (tok + 1, z)),
        remote(v.at[pl.ds(ROWS - HDIM, HDIM)], hv, hss.at[1], hrs.at[1], (tok + 1, z)),
    ]

    @pl.when(tok < 31)
    def _():
        for copy in halo:
            copy.start()

    @pl.when(tok == 0)
    def _():
        hk[...] = jnp.zeros_like(hk)
        hv[...] = jnp.zeros_like(hv)

    def before_rates(h):
        for copy in load_w[h]:
            copy.wait()
        columns = pl.ds(h * HDIM, HDIM)
        first = w1[h].astype(BF16)
        third = w3[h].astype(BF16)
        second = w2[h].astype(BF16)
        for part in range(2):
            rows = pl.ds(part * HDIM, HDIM)
            keys = k[rows, columns]
            values = v[rows, columns]
            kt[h, :, rows] = keys.T
            vt[h, :, rows] = values.T
            gate = dot(keys, first)
            up = dot(keys, third)
            back = -dot_nt(values, second)
            sig = jax.nn.sigmoid(gate)
            activ = gate * sig
            pg[h, rows, :] = back * up * sig * (1.0 + gate * (1.0 - sig))
            pu[h, rows, :] = back * activ
            hd[h, rows, :] = -(activ * up)

    for h in range(HEADS):
        before_rates(h)

    for copy in logit_copies:
        copy.wait_recv()
    logits = lg[z] + lrx[0] + lrx[1] + lrx[2]
    rates = jnp.maximum(logits, 0.0) + jnp.log1p(jnp.exp(-jnp.abs(logits)))
    rates_down = rates.T

    mine = pl.ds(pl.multiple_of(c * HALF, HALF), HALF)
    other = pl.ds(pl.multiple_of(HALF - c * HALF, HALF), HALF)

    s0 = [
        remote(gs0.at[m], rx0.at[m], ss0.at[m], rs0.at[m], sibling) for m in range(MATS)
    ]
    s1 = [None]
    for m in range(1, MATS):
        axis, place = PLACE[m]
        step = lax.rem(place - where[axis] + 4, 4)
        index = jnp.maximum(step - 1, 0)
        s1.append(
            [
                remote(
                    gs1.at[m, part], rx1.at[axis, index, part], ss1.at[m, i], rs1.at[axis, index, i],
                    on_axis(axis, place),
                )
                for i, part in enumerate(PARTS)
            ]
        )

    def quarter(place):
        return pl.ds(pl.multiple_of(place * QUARTER, QUARTER), QUARTER)

    my_quarter = quarter(c * 4 + x)
    every = [[], [], []]
    for d in (2, 1, 3):
        x_there, y_there = lax.rem(x + d, 4), lax.rem(y + d, 4)
        every[0].append(
            remote(gs1.at[0, quarter(x_there)], erx.at[0, d - 1], ess.at[0, d - 1], ers.at[0, d - 1], on_axis(0, x_there))
        )
        every[1].append(remote(es, erx.at[1, d - 1], ess.at[1, d - 1], ers.at[1, d - 1], on_axis(1, y_there)))
        every[2].append(
            remote(
                gfull.at[2, my_quarter], gfull.at[2, my_quarter], ess.at[2, d - 1], ers.at[2, d - 1], on_axis(0, x_there)
            )
        )

    def send_chip_sum(m):
        s0[m].wait_recv()
        both = gown[m] + rx0[m].astype(F32)
        gown[m] = both
        gs1[m] = both.astype(BF16)
        if m == 0:
            for copy in every[0]:
                copy.start()
            return
        axis, place = PLACE[m]

        @pl.when(where[axis] != place)
        def _():
            for copy in s1[m]:
                copy.start()

    for h in range(HEADS):
        rate = rates_down[:, h : h + 1]
        wides = ((kt, pg), (kt, pu), (vt, hd))
        for j, (left, right) in enumerate(wides):
            m = 3 * h + j
            scaled = (rate * right[h]).astype(BF16)
            whole[m % 2] = dot(left[h], scaled)
            gs0[m] = whole[m % 2, other, :].astype(BF16)
            s0[m].start()
            gown[m] = whole[m % 2, mine, :]
            if m >= LAG:
                send_chip_sum(m - LAG)
    for m in range(MATS - LAG, MATS):
        send_chip_sum(m)
    for copy in every[0]:
        copy.wait_recv()
    total = gown[0, quarter(x), :]
    for d in range(3):
        total = total + erx[0, d].astype(F32)
    eq[...] = total
    es[...] = total.astype(BF16)
    for copy in every[1]:
        copy.start()

    load_q.wait()

    @pl.when(tok > 0)
    def _():
        for copy in halo:
            copy.wait_recv()

    row = lax.broadcasted_iota(jnp.int32, (HDIM, HDIM), 0)
    column = lax.broadcasted_iota(jnp.int32, (HDIM, HDIM), 1)
    has_past = tok > 0

    def attend(h, carry):
        columns = pl.ds(pl.multiple_of(h * HDIM, HDIM), HDIM)
        low, high = pl.ds(0, HDIM), pl.ds(HDIM, HDIM)
        blocks = (
            (low, hk[:, columns], hv[:, columns], k[low, columns], v[low, columns], True),
            (high, k[low, columns], v[low, columns], k[high, columns], v[high, columns], False),
        )
        for rows, old_k, old_v, new_k, new_v, edge in blocks:
            queries = q[rows, columns]
            seen = column > row
            if edge:
                seen = jnp.logical_and(seen, has_past)
            old = jnp.where(seen, dot_nt(queries, old_k) * HDIM ** (-0.5), -1e30)
            new = jnp.where(column <= row, dot_nt(queries, new_k) * HDIM ** (-0.5), -1e30)
            top = jnp.maximum(jnp.max(old, axis=1, keepdims=True), jnp.max(new, axis=1, keepdims=True))
            old = jnp.exp(old - top)
            new = jnp.exp(new - top)
            total = jnp.sum(old, axis=1, keepdims=True) + jnp.sum(new, axis=1, keepdims=True)
            mixed = dot(old.astype(BF16), old_v) + dot(new.astype(BF16), new_v)
            att[rows, columns] = mixed / total
        return carry

    lax.fori_loop(0, HEADS, attend, 0)

    owned = (2 * x + 1, 2 * y + 2)
    second_copies = [
        [
            remote(
                gs2.at[slot, part], rx2.at[slot, d - 1, part], ss2.at[slot, d - 1, i], rs2.at[slot, d - 1, i],
                on_axis(1 - slot, lax.rem(where[1 - slot] + d, 4)),
            )
            for i, part in enumerate(PARTS)
            for d in (2, 1, 3)
        ]
        for slot in range(2)
    ]
    def my_part(i):
        return pl.ds(pl.multiple_of(c * HALF + i * PART, PART), PART)

    third_copies = [
        [
            remote(
                oall.at[owned[slot], my_part(i)], oall.at[owned[slot], my_part(i)],
                ss3.at[slot, d - 1, i], rs3.at[owned[slot], i], on_axis(slot, lax.rem(where[slot] + d, 4)),
            )
            for i in range(SPLIT)
            for d in (2, 1, 3)
        ]
        for slot in range(2)
    ]
    half_copies = [
        [
            remote(gfull.at[slot, my_part(i)], gfull.at[slot, my_part(i)], ssx.at[slot, i], rsx.at[slot, i], sibling)
            for i in range(SPLIT)
        ]
        for slot in range(2)
    ] + [[remote(gfull.at[2, mine], gfull.at[2, mine], ssx.at[2, 0], rsx.at[2, 0], sibling)]]

    def first_sum(slot, i):
        m, part = owned[slot], PARTS[i]
        total = gown[m, part, :]
        for d in range(3):
            remote(gs1.at[m, part], rx1.at[slot, d, part], ss1.at[m, i], rs1.at[slot, d, i], sibling).wait_recv()
            total = total + rx1[slot, d, part, :].astype(F32)
        gown[m, part, :] = total
        gs2[slot, part, :] = total.astype(BF16)
        for copy in second_copies[slot][3 * i : 3 * i + 3]:
            copy.start()

    def second_sum(slot, i):
        total = gown[owned[slot], PARTS[i], :]
        for copy in second_copies[slot][3 * i : 3 * i + 3]:
            copy.wait_recv()
        for d in range(3):
            total = total + rx2[slot, d, PARTS[i], :].astype(F32)
        gfull[slot, my_part(i), :] = total.astype(BF16)
        half_copies[slot][i].start()

    def orthogonalize(slots):
        iterates = []
        for slot in slots:
            for copy in half_copies[slot]:
                copy.wait_recv()
            full = gfull[slot].astype(F32)
            norm = jnp.sqrt(jnp.sum(full * full, keepdims=True)) + EPS_SCALE
            iterates.append((full / norm).astype(BF16))
        for repeat in range(STEPS):
            grams = [dot_nt(it, it).astype(BF16) for it in iterates]
            mixing = [
                (COEF_B * gram.astype(F32) + COEF_C * dot(gram, gram)).astype(BF16) for gram in grams
            ]
            iterates = [
                (COEF_A * it.astype(F32) + dot(mix, it)).astype(BF16) for mix, it in zip(mixing, iterates)
            ]
        for slot, it in zip(slots, iterates):
            oall[0 if slot == 2 else owned[slot]] = it

    for i in range(SPLIT):
        first_sum(0, i)
        first_sum(1, i)
    for copy in every[1]:
        copy.wait_recv()
    total = eq[...]
    for d in range(3):
        total = total + erx[1, d].astype(F32)
    gfull[2, my_quarter, :] = total.astype(BF16)
    for copy in every[2]:
        copy.start()
    for i in range(SPLIT):
        second_sum(0, i)
        second_sum(1, i)
    orthogonalize([0, 1])
    for pair in zip(*third_copies):
        for copy in pair:
            copy.start()
    for d in (2, 1, 3):
        theirs = quarter(c * 4 + lax.rem(x + 4 - d, 4))
        remote(gfull.at[2, theirs], gfull.at[2, theirs], ess.at[2, d - 1], ers.at[2, d - 1], sibling).wait_recv()
    half_copies[2][0].start()
    orthogonalize([2])

    fourth_copies = [None] + [
        [
            remote(oall.at[m, my_part(i)], oall.at[m, my_part(i)], ss4.at[m, i], rs4.at[m, i], sibling)
            for i in range(SPLIT)
        ]
        for m in range(1, MATS)
    ]

    def foreign(m, action):
        axis, place = PLACE[m]
        pl.when(where[axis] != place)(action)

    def forward(d, i):
        for m in (2 * lax.rem(x + d, 4) + 1, 2 * lax.rem(y + d, 4) + 2):
            part = oall.at[m, my_part(i)]
            remote(part, part, ss4.at[m, i], rs3.at[m, i], sibling).wait_recv()
            remote(part, part, ss4.at[m, i], rs4.at[m, i], sibling).start()

    def apply(h):
        for j in range(3):
            if 3 * h + j > 0:
                for copy in fourth_copies[3 * h + j]:
                    foreign(3 * h + j, copy.wait_recv)
        columns = pl.ds(h * HDIM, HDIM)
        size = scale_ref[h]
        first = (w1[h] - size * oall[3 * h].astype(F32)).astype(BF16)
        third = (w3[h] - size * oall[3 * h + 1].astype(F32)).astype(BF16)
        second = (w2[h] - size * oall[3 * h + 2].astype(F32).T).astype(BF16)
        gain = gain_ref[pl.ds(h * HDIM, HDIM)].reshape(1, HDIM)
        for part in range(2):
            rows = pl.ds(part * HDIM, HDIM)
            queries = q[rows, columns]
            gate = dot(queries, first)
            up = dot(queries, third)
            hidden = (gate * jax.nn.sigmoid(gate) * up).astype(BF16)
            fast = dot(hidden, second)
            spread = jnp.mean(fast * fast, axis=1, keepdims=True)
            normed = fast * lax.rsqrt(spread + EPS_RMS) * gain
            out_ref[rows, columns] = (att[rows, columns] + normed).astype(BF16)

    for i in range(SPLIT):
        for d in (1, 3, 2):
            forward(d, i)
    out_copies = []
    for h in range(HEADS):
        apply(h)
        columns = pl.ds(h * HDIM, HDIM)
        copy = pltpu.make_async_copy(out_ref.at[:, columns], out_hbm.at[:, columns], out_sem.at[h])
        copy.start()
        out_copies.append(copy)

    for copy in out_copies:
        copy.wait()
    for copy in logit_copies + s0:
        copy.wait_send()

    @pl.when(tok < 31)
    def _():
        for copy in halo:
            copy.wait_send()

    for m in range(1, MATS):
        for copy in s1[m] + fourth_copies[m]:
            foreign(m, copy.wait_send)
    for copies in every + second_copies + half_copies + third_copies:
        for copy in copies:
            copy.wait_send()


def on_device(x, rw, q, k, v, w1, w3, w2, scale, gain):
    anywhere = pl.BlockSpec(memory_space=pl.ANY)
    dma = pltpu.SemaphoreType.DMA
    features = x.shape[1]
    wide = HEADS * HDIM
    return pl.pallas_call(
        kernel,
        name="layer",
        out_shape=jax.ShapeDtypeStruct((ROWS, wide), BF16),
        in_specs=[anywhere] * 8
        + [pl.BlockSpec(memory_space=pltpu.SMEM), pl.BlockSpec(memory_space=pltpu.VMEM)],
        out_specs=anywhere,
        scratch_shapes=[
            pltpu.VMEM((ROWS, wide), BF16),
            dma((HEADS,)),
            pltpu.VMEM((ROWS, features), BF16),
            pltpu.VMEM((rw.shape[1], rw.shape[0]), BF16),
            pltpu.VMEM((ROWS, wide), BF16),
            pltpu.VMEM((ROWS, wide), BF16),
            pltpu.VMEM((ROWS, wide), BF16),
            pltpu.VMEM((HEADS, HDIM, FFN), F32),
            pltpu.VMEM((HEADS, HDIM, FFN), F32),
            pltpu.VMEM((HEADS, FFN, HDIM), F32),
            dma((14,)),
            pltpu.VMEM((ROWS, 128), F32),
            pltpu.VMEM((4, 8, ROWS), F32),
            pltpu.VMEM((3, 8, ROWS), F32),
            dma((3,)),
            dma((3,)),
            pltpu.VMEM((HDIM, wide), BF16),
            pltpu.VMEM((HDIM, wide), BF16),
            dma((2,)),
            dma((2,)),
            pltpu.VMEM((HEADS, ROWS, FFN), F32),
            pltpu.VMEM((HEADS, ROWS, FFN), F32),
            pltpu.VMEM((HEADS, ROWS, FFN), F32),
            pltpu.VMEM((HEADS, HDIM, ROWS), BF16),
            pltpu.VMEM((HEADS, HDIM, ROWS), BF16),
            pltpu.VMEM((ROWS, wide), F32),
            pltpu.VMEM((2, HDIM, FFN), F32),
            pltpu.VMEM((QUARTER, FFN), F32),
            pltpu.VMEM((QUARTER, FFN), BF16),
            pltpu.VMEM((2, 3, QUARTER, FFN), BF16),
            dma((3, 3)),
            dma((3, 3)),
            pltpu.VMEM((MATS, HALF, FFN), F32),
            pltpu.VMEM((MATS, HALF, FFN), BF16),
            pltpu.VMEM((MATS, HALF, FFN), BF16),
            pltpu.VMEM((MATS, HALF, FFN), BF16),
            pltpu.VMEM((2, 3, HALF, FFN), BF16),
            pltpu.VMEM((2, HALF, FFN), BF16),
            pltpu.VMEM((2, 3, HALF, FFN), BF16),
            pltpu.VMEM((3, HDIM, FFN), BF16),
            pltpu.VMEM((MATS, HDIM, FFN), BF16),
            dma((MATS,)),
            dma((MATS,)),
            dma((MATS, SPLIT)),
            dma((2, 3, SPLIT)),
            dma((2, 3, SPLIT)),
            dma((2, 3, SPLIT)),
            dma((3, SPLIT)),
            dma((3, SPLIT)),
            dma((2, 3, SPLIT)),
            dma((MATS, SPLIT)),
            dma((MATS, SPLIT)),
            dma((MATS, SPLIT)),
        ],
        compiler_params=pltpu.CompilerParams(
            collective_id=0, has_side_effects=True, vmem_limit_bytes=56 << 20
        ),
    )(x, rw.T, q, k, v, w1, w3, w2, scale, gain)


def solution(mesh):
    placed = (
        P("tok", "head"),
        P("head", None),
        P("tok", "head"),
        P("tok", "head"),
        P("tok", "head"),
        P("head", None, None),
        P("head", None, None),
        P("head", None, None),
        P("head"),
        P("head"),
    )
    return jax.shard_map(
        on_device, mesh=mesh, in_specs=placed, out_specs=P("tok", "head"), check_vma=False
    )
```
